32 devices in a mesh: blk: 8 (over z, x), pair: 4 (over y, core).
Axes of the slice: x: 2, y: 2, z: 4, core: 2. Of those that a mesh axis runs over, the one named last changes fastest.
Arguments:
- records: bfloat16 [8, 1024, 2048], P('blk', 'pair'), may hold values from -100 to 100
- offsets: int32 [2], replicated, may hold values from 1 to 7, as said below
- source_side: int32 [8, 2], P('blk'), may hold values from 0 to 1
Outputs:
- first_side: bfloat16 [8, 2, 32, 128, 128], P('blk', None, 'pair')
- second_side: bfloat16 [8, 2, 32, 128, 128], P('blk', None, 'pair')
The draws below stay inside these ranges and needn't reach their ends.
Inputs may be any that keep to these rules, and one draw needn't show every extreme that they name: `offsets`: distinct and increasing; the last one is 7.
All inputs are finite; a program needn't handle non-finite values.
Results may differ from the reference program's by a relative error of at most 0.012.
Values may be sent and summed in bfloat16 or wider, within the bound.
No kernel may reach another device: no remote copies, remote signals or barrier semaphores. Data moves between devices by JAX's collectives and lax.ppermute only.
A program may use at most 128 MiB of HBM per device.

```python
import math
import jax
import jax.numpy as jnp
from jax import lax

BLOCK_CH = 128
BINS = 128
SAMPLES = 2048
FIRST_BIN = 4
LAGS = 32
OFFSET_COUNT = 2
WINDOW = 8
SEGMENTS = 8
BLOCKS = 8
CHANNELS = 1024


def draw_records(key, part):
    base_key = jax.random.fold_in(key, 101)
    noise_key, channel_key, segment_key = jax.random.split(base_key, 3)
    channel_scale = jnp.exp(jax.random.uniform(channel_key, (1, CHANNELS, 1), jnp.float32, 0.0, math.log(10.0)))
    segment_scale = jnp.exp(jax.random.uniform(segment_key, (SEGMENTS, 1, 1), jnp.float32, 0.0, math.log(4.0)))
    noise = jax.random.normal(noise_key, (SEGMENTS, CHANNELS, SAMPLES), jnp.float32)
    values = noise * channel_scale * segment_scale
    return jnp.clip(values, -100.0, 100.0).astype(jnp.bfloat16)


def draw_offsets(key, part):
    order_key = jax.random.fold_in(key, 202)
    shuffled = jax.random.permutation(order_key, WINDOW - 2).astype(jnp.int32) + 1
    chosen = jnp.sort(shuffled[:OFFSET_COUNT - 1])
    last_one = jnp.full((1,), WINDOW - 1, jnp.int32)
    return jnp.concatenate([chosen, last_one]).astype(jnp.int32)


def plant(array, stream_key, smallest, top_value):
    longest = array.shape.index(max(array.shape))
    spots = []
    for shift in (0, 1):
        where = [jax.random.randint(jax.random.fold_in(stream_key, axis), (), 0, length) for axis, length in enumerate(array.shape)]
        where[longest] = (where[longest] + shift) % array.shape[longest]
        spots.append(tuple(where))
    return array.at[spots[0]].set(smallest).at[spots[1]].set(top_value)


def setup_inputs(seed: int = 0) -> dict:
    key_of = jax.random.split(jax.random.key(seed), 4)
    return {
        "records": draw_records(jax.random.fold_in(key_of[3], 71), 0),
        "offsets": draw_offsets(jax.random.fold_in(key_of[3], 71), 0),
        "source_side": plant(jax.random.randint(key_of[2], (BLOCKS, OFFSET_COUNT), 0, 2), jax.random.fold_in(key_of[2], 1), 0, 1).astype(jnp.int32),
    }


def whiten_segment(segment):
    sample_index = jnp.arange(SAMPLES, dtype=jnp.float32)
    hann_taper = 0.5 - 0.5 * jnp.cos(2.0 * math.pi / SAMPLES * sample_index)
    tapered = segment.astype(jnp.float32) * hann_taper
    spectrum = jnp.fft.rfft(tapered, axis=-1)[:, FIRST_BIN:FIRST_BIN + BINS]
    real_part = jnp.real(spectrum).reshape(BLOCKS, BLOCK_CH, BINS)
    imag_part = jnp.imag(spectrum).reshape(BLOCKS, BLOCK_CH, BINS)
    band_level = lax.optimization_barrier(jnp.mean(real_part * real_part + imag_part * imag_part, axis=1, keepdims=True))
    whiten_scale = 1.0 / jnp.sqrt(band_level + 1e-05)
    return jnp.stack((real_part * whiten_scale, imag_part * whiten_scale)).astype(jnp.bfloat16)

def reference(records, offsets, source_side):
    whitened = lax.map(whiten_segment, records)
    lag_index = jnp.arange(LAGS, dtype=jnp.int32) - LAGS // 2
    bin_index = FIRST_BIN + jnp.arange(BINS, dtype=jnp.int32)
    phase_index = lag_index[:, None] * bin_index[None, :] % SAMPLES
    angles = 2.0 * math.pi / SAMPLES * phase_index.astype(jnp.float32)
    normalizer = 1.0 / jnp.sqrt(jnp.float32(SEGMENTS * BINS))
    cos_table = jnp.cos(angles) * normalizer
    sin_table = jnp.sin(angles) * normalizer
    highest = lax.Precision.HIGHEST

    def pair_block(block_index):
        own_block = lax.dynamic_index_in_dim(whitened, block_index, axis=2, keepdims=False)
        results = []
        for offset_slot in range(OFFSET_COUNT):
            partner = block_index + offsets[offset_slot]
            in_range = partner < BLOCKS
            partner_block = lax.dynamic_index_in_dim(whitened, jnp.minimum(partner, BLOCKS - 1).astype(jnp.int32), axis=2, keepdims=False)
            reverse_side = source_side[block_index, offset_slot] == 1
            source = jnp.where(reverse_side, partner_block, own_block).astype(jnp.float32)
            receiver = jnp.where(reverse_side, own_block, partner_block).astype(jnp.float32)
            cross_real = jnp.einsum('scf,sdf->fcd', source[:, 0], receiver[:, 0], precision=highest) + jnp.einsum('scf,sdf->fcd', source[:, 1], receiver[:, 1], precision=highest)
            cross_imag = jnp.einsum('scf,sdf->fcd', source[:, 0], receiver[:, 1], precision=highest) - jnp.einsum('scf,sdf->fcd', source[:, 1], receiver[:, 0], precision=highest)
            lagged = jnp.einsum('lf,fcd->lcd', cos_table, cross_real, precision=highest) - jnp.einsum('lf,fcd->lcd', sin_table, cross_imag, precision=highest)
            results.append(jnp.where(in_range, lagged, jnp.zeros_like(lagged)).astype(jnp.bfloat16))
        return jnp.stack(results)
    first_side = lax.map(pair_block, jnp.arange(BLOCKS, dtype=jnp.int32))
    seconds = []
    for offset_slot in range(OFFSET_COUNT):
        anchor = jnp.arange(BLOCKS, dtype=jnp.int32) - offsets[offset_slot]
        picked = jnp.take(first_side[:, offset_slot], jnp.maximum(anchor, 0).astype(jnp.int32), axis=0)
        seconds.append(jnp.where((anchor >= 0)[:, None, None, None], picked, jnp.zeros_like(picked)))
    second_side = jnp.stack(seconds, axis=1)
    return (first_side, second_side)
```

```python
import math

import jax
import jax.numpy as jnp
import numpy as np
from jax import lax
from jax.experimental import pallas as pl
from jax.experimental.pallas import tpu as pltpu
from jax.sharding import PartitionSpec as P

BLOCK_CH = 128
BINS = 128
SAMPLES = 2048
FIRST_BIN = 4
LAGS = 32
HALF_CH = BLOCK_CH // 2
BLOCKS_PER_STEP = 2
SEGS_PER_STEP = 8
FLAG_ROWS = 8
SLOT_ROWS = 2 * HALF_CH


def fourier_table():
    sample_index = np.arange(SAMPLES)
    bin_index = FIRST_BIN + np.arange(BINS)
    angles = 2.0 * math.pi / SAMPLES * (sample_index[:, None] * bin_index[None, :] % SAMPLES)
    hann_taper = 0.5 - 0.5 * np.cos(2.0 * math.pi / SAMPLES * sample_index)
    full = np.concatenate(
        (hann_taper[:, None] * np.cos(angles), -hann_taper[:, None] * np.sin(angles)), axis=1
    ).astype(np.float32)
    high = full.astype(jnp.bfloat16)
    low = (full - high.astype(np.float32)).astype(jnp.bfloat16)
    return np.concatenate((high, low), axis=1)


def lag_tables():
    lag_index = np.arange(LAGS) - LAGS // 2
    bin_index = FIRST_BIN + np.arange(BINS)
    angles = 2.0 * math.pi / SAMPLES * (lag_index[:, None] * bin_index[None, :] % SAMPLES)
    return np.cos(angles).astype(np.float32), np.sin(angles).astype(np.float32)


def whiten(records, half_of):
    blocks = records.shape[0] // BLOCK_CH
    step_blocks = min(BLOCKS_PER_STEP, blocks)

    def kernel(records_ref, table_ref, mine_ref, other_ref, held):
        half = half_of(lax.axis_index("pair"))
        both = jnp.dot(records_ref[...], table_ref[...], preferred_element_type=jnp.float32)
        spectrum = both[:, : 2 * BINS] + both[:, 2 * BINS :]
        for block in range(step_blocks):
            part = spectrum[block * BLOCK_CH : (block + 1) * BLOCK_CH]
            real, imag = part[:, :BINS], part[:, BINS:]
            level = jnp.mean(real * real + imag * imag, axis=0, keepdims=True)
            scale = 1.0 / jnp.sqrt(level + 1e-05)
            for index, value in enumerate((real * scale, imag * scale)):
                rounded = value.astype(jnp.bfloat16)
                held[block, 0, index] = rounded[:HALF_CH]
                held[block, 1, index] = rounded[HALF_CH:]
            mine_ref[block] = held[block, half]
            other_ref[block] = held[block, 1 - half]

    shape = (blocks, 2, HALF_CH, BINS)
    spec = pl.BlockSpec((step_blocks,) + shape[1:], lambda b: (b, 0, 0, 0))
    return pl.pallas_call(
        kernel,
        grid=(blocks // step_blocks,),
        in_specs=[
            pl.BlockSpec((step_blocks * BLOCK_CH, SAMPLES), lambda b: (b, 0)),
            pl.BlockSpec((SAMPLES, 4 * BINS), lambda b: (0, 0)),
        ],
        out_specs=[spec, spec],
        out_shape=[jax.ShapeDtypeStruct(shape, jnp.bfloat16)] * 2,
        scratch_shapes=[pltpu.VMEM((step_blocks, 2, 2, HALF_CH, BINS), jnp.bfloat16)],
        name="whiten",
    )(records, jnp.asarray(fourier_table()))


def partner_of(row, slot, offset_at, group, offset_total):
    if group_is_window(group) and offset_total == 2:
        last = group - 1
        if slot == 0:
            ahead = row + offset_at(0)
            return jnp.where(ahead < group, ahead, row - last)
        behind = row - offset_at(0)
        return jnp.where(behind >= 0, behind, row + last)
    step = offset_at(slot % offset_total)
    return row + step if slot < offset_total else row - step


def group_is_window(group):
    return group <= 16


def slot_total(group, offset_total):
    return 2 if group_is_window(group) and offset_total == 2 else 2 * offset_total


def slot_of(row, side, k, offset_at, group, offset_total):
    if group_is_window(group) and offset_total == 2:
        if k == 0:
            return side
        return jnp.where(row == 0, 1, 0)
    return side * offset_total + k


def pack(pieces, offsets, source_side, group):
    offset_total = offsets.shape[0]
    slots = slot_total(group, offset_total)
    piece_blocks = pieces[0].shape[0]
    rows = (1 + slots) * SLOT_ROWS

    def kernel(offsets_ref, side_ref, *refs):
        piece_refs, out_ref, held = refs[: len(pieces)], refs[-2], refs[-1]
        pair = lax.axis_index("pair")
        for turn, piece_ref in enumerate(piece_refs):
            first = (pair ^ turn) * piece_blocks
            for block in range(piece_blocks):
                held[first + block] = piece_ref[block].reshape(SLOT_ROWS, BINS)
        lane = lax.broadcasted_iota(jnp.int32, (FLAG_ROWS, BINS), 1)
        flags = jnp.zeros((FLAG_ROWS, BINS), jnp.float32)
        for k in range(offset_total):
            flags = jnp.where(lane == k, side_ref[0, k].astype(jnp.float32), flags)
        flags = flags.astype(jnp.bfloat16)

        def fill(row, carry):
            out_ref[row, :SLOT_ROWS] = held[row]
            for slot in range(slots):
                partner = partner_of(row, slot, lambda k: offsets_ref[k], group, offset_total)
                partner = jnp.clip(partner, 0, group - 1)
                out_ref[row, (slot + 1) * SLOT_ROWS : (slot + 2) * SLOT_ROWS] = held[partner]
            out_ref[row, rows:] = flags
            return carry

        lax.fori_loop(0, group, fill, 0)

    smem = pl.BlockSpec(memory_space=pltpu.SMEM)
    vmem = pl.BlockSpec(memory_space=pltpu.VMEM)
    return pl.pallas_call(
        kernel,
        in_specs=[smem, smem] + [vmem] * len(pieces),
        out_specs=vmem,
        out_shape=jax.ShapeDtypeStruct((group, rows + FLAG_ROWS, BINS), jnp.bfloat16),
        scratch_shapes=[pltpu.VMEM((group, SLOT_ROWS, BINS), jnp.bfloat16)],
        name="pack",
    )(offsets, source_side, *pieces)


def correlate(mine, theirs, offsets, source_side, group, lag_local, half_of):
    offset_total = offsets.shape[0]
    slots = slot_total(group, offset_total)
    segs = mine.shape[0]
    steps = segs // SEGS_PER_STEP
    depth = SEGS_PER_STEP * 2 * BINS
    normalizer = 1.0 / math.sqrt(segs * BINS)
    flag_row = (1 + slots) * SLOT_ROWS

    def kernel(
        offsets_ref, side_ref, flags_ref, cos_ref, sin_ref, mine_ref, theirs_ref,
        first_ref, second_ref, left, right, total,
    ):
        slab, step = pl.program_id(0), pl.program_id(1)
        row, pair = lax.axis_index("blk"), lax.axis_index("pair")
        half = half_of(pair)
        side, k = slab // offset_total, slab % offset_total
        other = jnp.where(side == 0, row + offsets_ref[k], row - offsets_ref[k])
        valid = jnp.logical_and(other >= 0, other < group)
        lane = lax.broadcasted_iota(jnp.int32, (FLAG_ROWS, BINS), 1)
        flag_seg = jnp.clip(other, 0, group - 1)
        far_flags = flags_ref[flag_seg].astype(jnp.float32)
        far_side = jnp.max(jnp.where(lane == k, far_flags, 0.0)) > 0.5
        swapped = jnp.where(side == 0, side_ref[0, k] == 1, jnp.logical_not(far_side))
        slot = 0
        for a_side in range(2):
            for a_k in range(offset_total):
                here = slot_of(row, a_side, a_k, lambda j: offsets_ref[j], group, offset_total)
                slot = jnp.where(slab == a_side * offset_total + a_k, here, slot)
        slot = slot + 1
        source = pl.multiple_of(jnp.where(swapped, slot, 0) * SLOT_ROWS, SLOT_ROWS)
        receiver = pl.multiple_of(jnp.where(swapped, 0, slot) * SLOT_ROWS, SLOT_ROWS)

        def emit(value):
            value = value.reshape(1, 1, lag_local, BLOCK_CH, BLOCK_CH)

            @pl.when(side == 0)
            def _():
                first_ref[...] = value

            @pl.when(side != 0)
            def _():
                second_ref[...] = value

        @pl.when(jnp.logical_not(valid))
        def _():
            emit(jnp.zeros((lag_local, BLOCK_CH, BLOCK_CH), jnp.bfloat16))

        @pl.when(valid)
        def _():
            lag_rows = pl.ds(pl.multiple_of(pair * lag_local, lag_local), lag_local)
            cosines, sines = cos_ref[lag_rows], sin_ref[lag_rows]
            for seg in range(SEGS_PER_STEP):
                at = seg * 2 * BINS
                for which, ref in ((half, mine_ref), (1 - half, theirs_ref)):
                    top = pl.multiple_of(which * HALF_CH, HALF_CH)
                    for part in range(2):
                        right[pl.ds(top, HALF_CH), at + part * BINS : at + (part + 1) * BINS] = ref[
                            seg, pl.ds(receiver + part * HALF_CH, HALF_CH)
                        ]
                    real = ref[seg, pl.ds(source, HALF_CH)].astype(jnp.float32)
                    imag = ref[seg, pl.ds(source + HALF_CH, HALF_CH)].astype(jnp.float32)
                    for lag in range(lag_local):
                        c, s = cosines[lag : lag + 1], sines[lag : lag + 1]
                        rows = pl.ds(lag * BLOCK_CH + top, HALF_CH)
                        left[rows, at : at + BINS] = (real * c + imag * s).astype(jnp.bfloat16)
                        left[rows, at + BINS : at + 2 * BINS] = (imag * c - real * s).astype(
                            jnp.bfloat16
                        )
            product = lax.dot_general(
                left[...], right[...], (((1,), (1,)), ((), ())), preferred_element_type=jnp.float32
            )
            if steps == 1:
                emit((product * normalizer).astype(jnp.bfloat16))
            else:

                @pl.when(step == 0)
                def _():
                    total[...] = product

                @pl.when(step > 0)
                def _():
                    total[...] += product

                @pl.when(step == steps - 1)
                def _():
                    emit((total[...] * normalizer).astype(jnp.bfloat16))

    smem = pl.BlockSpec(memory_space=pltpu.SMEM)
    vmem = pl.BlockSpec(memory_space=pltpu.VMEM)
    chunk = pl.BlockSpec((SEGS_PER_STEP,) + mine.shape[1:], lambda a, b: (b, 0, 0))
    out_shape = (1, offset_total, lag_local, BLOCK_CH, BLOCK_CH)
    out_block = (1, 1) + out_shape[2:]
    cos_table, sin_table = lag_tables()
    flag_block = flag_row // FLAG_ROWS
    return pl.pallas_call(
        kernel,
        grid=(2 * offset_total, steps),
        in_specs=[
            smem,
            smem,
            pl.BlockSpec((segs, FLAG_ROWS, BINS), lambda a, b: (0, flag_block, 0)),
            vmem,
            vmem,
            chunk,
            chunk,
        ],
        out_specs=[
            pl.BlockSpec(out_block, lambda a, b: (0, jnp.minimum(a, offset_total - 1), 0, 0, 0)),
            pl.BlockSpec(out_block, lambda a, b: (0, jnp.maximum(a - offset_total, 0), 0, 0, 0)),
        ],
        out_shape=[jax.ShapeDtypeStruct(out_shape, jnp.bfloat16)] * 2,
        scratch_shapes=[
            pltpu.VMEM((lag_local * BLOCK_CH, depth), jnp.bfloat16),
            pltpu.VMEM((BLOCK_CH, depth), jnp.bfloat16),
            pltpu.VMEM((lag_local * BLOCK_CH, BLOCK_CH), jnp.float32),
        ],
        name="correlate",
    )(offsets, source_side, mine, jnp.asarray(cos_table), jnp.asarray(sin_table), mine, theirs)


def local(records, offsets, source_side):
    group, pairs = lax.axis_size("blk"), lax.axis_size("pair")
    half_of = lambda pair: pair % 2
    assert records.shape[0] == 1
    swap = lambda value, turn: lax.ppermute(value, "pair", [(a, a ^ turn) for a in range(pairs)])
    mine, other = whiten(records.reshape(records.shape[0] * records.shape[1], SAMPLES), half_of)
    pieces = [mine] + [swap(other if turn % 2 else mine, turn) for turn in range(1, pairs)]
    packed = pack(pieces, offsets, source_side, group)
    arrived = lax.all_to_all(packed, "blk", split_axis=0, concat_axis=0, tiled=True)
    arrived_other = swap(arrived, 1)
    first, second = correlate(
        arrived, arrived_other, offsets, source_side, group, LAGS // pairs, half_of
    )
    return first, second


def solution(mesh):
    placed = (P("blk", "pair", None), P(), P("blk", None))
    return jax.shard_map(
        local,
        mesh=mesh,
        in_specs=placed,
        out_specs=(P("blk", None, "pair", None, None), P("blk", None, "pair", None, None)),
        check_vma=False,
    )
```

```python
import math

import jax
import jax.numpy as jnp
import numpy as np
from jax import lax
from jax.experimental import pallas as pl
from jax.experimental.pallas import tpu as pltpu
from jax.sharding import PartitionSpec as P

BLOCK_CH = 128
BINS = 128
SAMPLES = 2048
FIRST_BIN = 4
LAGS = 32
HALF_CH = BLOCK_CH // 2
BLOCKS_PER_STEP = 2
SEGS_PER_STEP = 8
FLAG_ROWS = 8
SLOT_ROWS = 2 * HALF_CH


def fourier_table():
    sample_index = np.arange(SAMPLES)
    bin_index = FIRST_BIN + np.arange(BINS)
    angles = 2.0 * math.pi / SAMPLES * (sample_index[:, None] * bin_index[None, :] % SAMPLES)
    hann_taper = 0.5 - 0.5 * np.cos(2.0 * math.pi / SAMPLES * sample_index)
    full = np.concatenate(
        (hann_taper[:, None] * np.cos(angles), -hann_taper[:, None] * np.sin(angles)), axis=1
    ).astype(np.float32)
    high = full.astype(jnp.bfloat16)
    low = (full - high.astype(np.float32)).astype(jnp.bfloat16)
    return np.concatenate((high, low), axis=1)


def lag_tables(pairs):
    theta = 2.0 * math.pi / SAMPLES * (FIRST_BIN + np.arange(BINS))
    lag_local = LAGS // pairs
    middle = np.arange(pairs) * lag_local + lag_local // 2 - LAGS // 2
    away = np.arange(1, lag_local // 2 + 1)
    tables = [f(lags[:, None] * theta[None]) for lags in (middle, away) for f in (np.cos, np.sin)]
    return [jnp.asarray(table.astype(np.float32)) for table in tables]


def whiten(records, half_of):
    blocks = records.shape[0] // BLOCK_CH
    step_blocks = min(BLOCKS_PER_STEP, blocks)

    def kernel(records_ref, table_ref, mine_ref, other_ref, held):
        half = half_of(lax.axis_index("pair"))
        both = jnp.dot(records_ref[...], table_ref[...], preferred_element_type=jnp.float32)
        spectrum = both[:, : 2 * BINS] + both[:, 2 * BINS :]
        for block in range(step_blocks):
            part = spectrum[block * BLOCK_CH : (block + 1) * BLOCK_CH]
            real, imag = part[:, :BINS], part[:, BINS:]
            level = jnp.mean(real * real + imag * imag, axis=0, keepdims=True)
            scale = 1.0 / jnp.sqrt(level + 1e-05)
            for index, value in enumerate((real * scale, imag * scale)):
                rounded = value.astype(jnp.bfloat16)
                held[block, 0, index] = rounded[:HALF_CH]
                held[block, 1, index] = rounded[HALF_CH:]
            mine_ref[block] = held[block, half]
            other_ref[block] = held[block, 1 - half]

    shape = (blocks, 2, HALF_CH, BINS)
    spec = pl.BlockSpec((step_blocks,) + shape[1:], lambda b: (b, 0, 0, 0))
    return pl.pallas_call(
        kernel,
        grid=(blocks // step_blocks,),
        in_specs=[
            pl.BlockSpec((step_blocks * BLOCK_CH, SAMPLES), lambda b: (b, 0)),
            pl.BlockSpec((SAMPLES, 4 * BINS), lambda b: (0, 0)),
        ],
        out_specs=[spec, spec],
        out_shape=[jax.ShapeDtypeStruct(shape, jnp.bfloat16)] * 2,
        scratch_shapes=[pltpu.VMEM((step_blocks, 2, 2, HALF_CH, BINS), jnp.bfloat16)],
        name="whiten",
    )(records, jnp.asarray(fourier_table()))


def group_is_window(group, offset_total):
    return group <= 16 and offset_total == 2


def slot_total(group, offset_total):
    return 2 if group_is_window(group, offset_total) else 2 * offset_total


def slot_pair(row, slot, offset_at, group, offset_total):
    if group_is_window(group, offset_total):
        last = group - 1
        if slot == 0:
            ahead = row + offset_at(0)
            inside = ahead < group
            return jnp.where(inside, 0, 1), jnp.where(inside, 0, 1), jnp.where(inside, ahead, row - last)
        behind = row - offset_at(0)
        inside = behind >= 0
        return jnp.where(inside, 1, 0), jnp.where(inside, 0, 1), jnp.where(inside, behind, row + last)
    side, k = slot // offset_total, slot % offset_total
    return side, k, row - offset_at(k) if side else row + offset_at(k)


def in_vmem(value):
    return pltpu.with_memory_space_constraint(value, pltpu.VMEM)


SMEM_SPEC = pl.BlockSpec(memory_space=pltpu.SMEM)
VMEM_SPEC = pl.BlockSpec(memory_space=pltpu.VMEM)


def pack(pieces, offsets, source_side, group, by_turn):
    offset_total = offsets.shape[0]
    slots = slot_total(group, offset_total)
    piece_blocks = pieces[0].shape[0]
    rows = (1 + slots) * SLOT_ROWS

    def kernel(offsets_ref, side_ref, *refs):
        piece_refs, out_refs, held = refs[: len(pieces)], refs[len(pieces) : -1], refs[-1]
        own_row, pair = lax.axis_index("blk"), lax.axis_index("pair")
        for turn, piece_ref in enumerate(piece_refs):
            first = (pair ^ turn) * piece_blocks
            for block in range(piece_blocks):
                held[first + block] = piece_ref[block].reshape(SLOT_ROWS, BINS)
        lane = lax.broadcasted_iota(jnp.int32, (FLAG_ROWS, BINS), 1)
        flags = jnp.zeros((FLAG_ROWS, BINS), jnp.float32)
        for k in range(offset_total):
            flags = jnp.where(lane == k, side_ref[0, k].astype(jnp.float32), flags)
        flags = flags.astype(jnp.bfloat16)

        def fill(row, out_ref):
            out_ref[:SLOT_ROWS] = held[row]
            for slot in range(slots):
                _, _, partner = slot_pair(row, slot, lambda k: offsets_ref[k], group, offset_total)
                partner = jnp.clip(partner, 0, group - 1)
                out_ref[(slot + 1) * SLOT_ROWS : (slot + 2) * SLOT_ROWS] = held[partner]
            out_ref[rows:] = flags

        if by_turn:
            for turn, out_ref in enumerate(out_refs):
                fill(own_row ^ turn, out_ref)
        else:

            @pl.loop(0, group)
            def _(row):
                fill(row, out_refs[0].at[row])

    shape = (rows + FLAG_ROWS, BINS)
    if by_turn:
        out_shape = [pltpu.VMEM(shape, jnp.bfloat16)] * group
    else:
        out_shape = [jax.ShapeDtypeStruct((group,) + shape, jnp.bfloat16)]
    return pl.pallas_call(
        kernel,
        in_specs=[SMEM_SPEC, SMEM_SPEC] + [VMEM_SPEC] * len(pieces),
        out_specs=[VMEM_SPEC] * len(out_shape),
        out_shape=out_shape,
        scratch_shapes=[pltpu.VMEM((group, SLOT_ROWS, BINS), jnp.bfloat16)],
        name="pack",
    )(offsets, source_side, *[in_vmem(piece) for piece in pieces])


def correlate(mine, theirs, offsets, source_side, group, pairs, half_of):
    offset_total = offsets.shape[0]
    slots = slot_total(group, offset_total)
    by_turn = isinstance(mine, list)
    segs = len(mine) if by_turn else mine.shape[0]
    chunk = segs if by_turn else SEGS_PER_STEP
    steps = segs // chunk
    lag_local = LAGS // pairs
    span = lag_local // 2
    left_rows, right_rows = (2 * span + 1) * BLOCK_CH, 2 * BLOCK_CH
    normalizer = 1.0 / math.sqrt(segs * BINS)
    flag_row = (1 + slots) * SLOT_ROWS
    count = chunk if by_turn else 1

    def kernel(offsets_ref, side_ref, cos_mid, sin_mid, cos_away, sin_away, *refs):
        mine_refs, theirs_refs, refs = refs[:count], refs[count : 2 * count], refs[2 * count :]
        if by_turn:
            seg_refs = list(zip(mine_refs, theirs_refs))
        else:
            flags_ref, refs = refs[0], refs[1:]
            seg_refs = [(mine_refs[0].at[a], theirs_refs[0].at[a]) for a in range(chunk)]
        first_ref, second_ref, left, right, total = refs
        duo, step = pl.program_id(0), pl.program_id(1)
        row, pair = lax.axis_index("blk"), lax.axis_index("pair")
        half = half_of(pair)
        lane = lax.broadcasted_iota(jnp.int32, (FLAG_ROWS, BINS), 1)

        def far_side(other, k):
            if by_turn:
                flags = jnp.zeros((FLAG_ROWS, BINS), jnp.float32)
                for turn, (ref, _) in enumerate(seg_refs):
                    piece = ref[flag_row:].astype(jnp.float32)
                    flags = jnp.where(row ^ turn == other, piece, flags)
            else:
                flags = flags_ref[other].astype(jnp.float32)
            return jnp.max(jnp.where(lane == k, flags, 0.0)) > 0.5

        lanes = []
        for a in range(2):
            side, k, other = 0, 0, 0
            for b in range(slots // 2):
                found = slot_pair(row, 2 * b + a, lambda j: offsets_ref[j], group, offset_total)
                side, k, other = [jnp.where(duo == b, x, y) for x, y in zip(found, (side, k, other))]
            valid = jnp.logical_and(other >= 0, other < group)
            far = far_side(jnp.clip(other, 0, group - 1), k)
            own_source = jnp.where(side == 0, side_ref[0, k] == 0, far)
            start = pl.multiple_of((2 * duo + a + 1) * SLOT_ROWS, SLOT_ROWS)
            lanes.append((side, k, valid, own_source, jnp.where(own_source, 1.0, -1.0), start))

        @pl.when(jnp.logical_and(duo == 0, step == 0))
        def _():
            first_ref[...] = jnp.zeros_like(first_ref)
            second_ref[...] = jnp.zeros_like(second_ref)

        @pl.when(jnp.logical_or(lanes[0][2], lanes[1][2]))
        def _():
            c_mid, s_mid = cos_mid[pl.ds(pair, 1)], sin_mid[pl.ds(pair, 1)]
            c_away, s_away = cos_away[...], sin_away[...]
            for seg, seg_pair in enumerate(seg_refs):
                for which, ref in zip((half, 1 - half), seg_pair):
                    top = pl.multiple_of(which * HALF_CH, HALF_CH)

                    def put(target, part, block, value):
                        rows = pl.ds(block * BLOCK_CH + top, HALF_CH)
                        target[2 * seg + part, rows] = value.astype(jnp.bfloat16)

                    real, imag = ref[:HALF_CH], ref[HALF_CH : 2 * HALF_CH]
                    put(left, 0, 0, real)
                    put(left, 1, 0, imag)
                    real, imag = real.astype(jnp.float32), imag.astype(jnp.float32)
                    for m in range(span):
                        c, s = c_away[m : m + 1], s_away[m : m + 1]
                        put(left, 0, 1 + m, real * c)
                        put(left, 1, 1 + m, imag * c)
                        put(left, 0, 1 + span + m, -(imag * s))
                        put(left, 1, 1 + span + m, real * s)
                    for a, (_, _, _, _, sign, start) in enumerate(lanes):
                        real = ref[pl.ds(start, HALF_CH)].astype(jnp.float32)
                        imag = ref[pl.ds(start + HALF_CH, HALF_CH)].astype(jnp.float32)
                        s = s_mid * sign
                        put(right, 0, a, real * c_mid - imag * s)
                        put(right, 1, a, imag * c_mid + real * s)
            product = lax.dot_general(
                jnp.concatenate([left[a] for a in range(2 * chunk)], axis=1),
                jnp.concatenate([right[a] for a in range(2 * chunk)], axis=1),
                (((1,), (1,)), ((), ())),
                preferred_element_type=jnp.float32,
            )
            if steps == 1:
                total[...] = product
            else:

                @pl.when(step == 0)
                def _():
                    total[...] = product

                @pl.when(step > 0)
                def _():
                    total[...] += product

        for a, (side, k, valid, own_source, sign, _) in enumerate(lanes):

            def emit(out_ref, turned):
                columns = slice(a * BLOCK_CH, (a + 1) * BLOCK_CH)
                for lag in range(lag_local):
                    m = abs(lag - span)
                    value = total[m * BLOCK_CH : (m + 1) * BLOCK_CH, columns]
                    if m:
                        at = (span + m) * BLOCK_CH
                        odd = total[at : at + BLOCK_CH, columns]
                        add = (lag < span) != turned
                        value = value + odd if add else value - odd
                    value = value * normalizer
                    out_ref[0, k, lag] = (value.T if turned else value).astype(jnp.bfloat16)

            for a_side, out_ref in enumerate((first_ref, second_ref)):
                for turned in (False, True):
                    here = jnp.logical_and(valid, step == steps - 1)
                    here = jnp.logical_and(here, side == a_side)
                    here = jnp.logical_and(here, own_source != turned)

                    @pl.when(here)
                    def _():
                        emit(out_ref, turned)

    out_shape = (1, offset_total, lag_local, BLOCK_CH, BLOCK_CH)
    out_spec = pl.BlockSpec(out_shape, lambda a, b: (0, 0, 0, 0, 0))
    if by_turn:
        operands = [in_vmem(piece) for piece in mine + theirs]
        specs = [VMEM_SPEC] * len(operands)
    else:
        flag_block = flag_row // FLAG_ROWS
        piece = pl.BlockSpec((chunk,) + mine.shape[1:], lambda a, b: (b, 0, 0))
        operands = [mine, theirs, mine]
        specs = [piece, piece, pl.BlockSpec((segs, FLAG_ROWS, BINS), lambda a, b: (0, flag_block, 0))]
    return pl.pallas_call(
        kernel,
        grid=(slots // 2, steps),
        in_specs=[SMEM_SPEC, SMEM_SPEC] + [VMEM_SPEC] * 4 + specs,
        out_specs=[out_spec] * 2,
        out_shape=[jax.ShapeDtypeStruct(out_shape, jnp.bfloat16)] * 2,
        scratch_shapes=[
            pltpu.VMEM((2 * chunk, left_rows, BINS), jnp.bfloat16),
            pltpu.VMEM((2 * chunk, right_rows, BINS), jnp.bfloat16),
            pltpu.VMEM((left_rows, right_rows), jnp.float32),
        ],
        name="correlate",
    )(offsets, source_side, *lag_tables(pairs), *operands)


def local(records, offsets, source_side):
    group, pairs = lax.axis_size("blk"), lax.axis_size("pair")
    half_of = lambda pair: pair % 2
    assert records.shape[0] == 1

    def swap(value, axis, turn):
        return lax.ppermute(value, axis, [(a, a ^ turn) for a in range(lax.axis_size(axis))])

    mine, other = whiten(records.reshape(records.shape[1], SAMPLES), half_of)
    pieces = [mine] + [swap(other if turn % 2 else mine, "pair", turn) for turn in range(1, pairs)]
    by_turn = group <= 8
    packed = pack(pieces, offsets, source_side, group, by_turn)
    if by_turn:
        arrived = [swap(value, "blk", turn) if turn else value for turn, value in enumerate(packed)]
        arrived_other = [swap(value, "pair", 1) for value in arrived]
    else:
        arrived = lax.all_to_all(packed[0], "blk", split_axis=0, concat_axis=0, tiled=True)
        arrived_other = swap(arrived, "pair", 1)
    return correlate(arrived, arrived_other, offsets, source_side, group, pairs, half_of)


def solution(mesh):
    placed = (P("blk", "pair", None), P(), P("blk", None))
    return jax.shard_map(
        local,
        mesh=mesh,
        in_specs=placed,
        out_specs=(P("blk", None, "pair", None, None), P("blk", None, "pair", None, None)),
        check_vma=False,
    )
```

```python
import math

import jax
import jax.numpy as jnp
import numpy as np
from jax import lax
from jax.experimental import pallas as pl
from jax.experimental.pallas import tpu as pltpu
from jax.sharding import PartitionSpec as P

BLOCK_CH = 128
BINS = 128
SAMPLES = 2048
FIRST_BIN = 4
LAGS = 32
HALF_CH = BLOCK_CH // 2
BLOCKS_PER_STEP = 2
DEPTH_CHUNKS = 4
TURNS = (0, 4, 5, 6, 7, 2, 3, 1)
SEGS_PER_STEP = 8
FLAG_ROWS = 8
SLOT_ROWS = 2 * HALF_CH
SMEM_SPEC = pl.BlockSpec(memory_space=pltpu.SMEM)
VMEM_SPEC = pl.BlockSpec(memory_space=pltpu.VMEM)


def fourier_table():
    sample_index = np.arange(SAMPLES)
    bin_index = FIRST_BIN + np.arange(BINS)
    angles = 2.0 * math.pi / SAMPLES * (sample_index[:, None] * bin_index[None, :] % SAMPLES)
    hann_taper = 0.5 - 0.5 * np.cos(2.0 * math.pi / SAMPLES * sample_index)
    full = np.concatenate(
        (hann_taper[:, None] * np.cos(angles), -hann_taper[:, None] * np.sin(angles)), axis=1
    ).astype(np.float32)
    high = full.astype(jnp.bfloat16)
    low = (full - high.astype(np.float32)).astype(jnp.bfloat16)
    return np.concatenate((high, low), axis=1)


def lag_tables(pairs):
    theta = 2.0 * math.pi / SAMPLES * (FIRST_BIN + np.arange(BINS))
    lag_local = LAGS // pairs
    middle = np.arange(pairs) * lag_local + lag_local // 2 - LAGS // 2
    away = np.arange(1, lag_local // 2 + 1)
    tables = [f(lags[:, None] * theta[None]) for lags in (middle, away) for f in (np.cos, np.sin)]
    return [jnp.asarray(table.astype(np.float32)) for table in tables]


def whiten(records, half_of):
    blocks = records.shape[0] // BLOCK_CH
    step_blocks = min(BLOCKS_PER_STEP, blocks)
    step_rows = step_blocks * BLOCK_CH
    depth = SAMPLES // DEPTH_CHUNKS

    def kernel(records_hbm, table_hbm, mine_ref, other_ref, held, traces, table, trace_sem, table_sem):
        step = pl.program_id(0)
        half = half_of(lax.axis_index("pair"))

        def trace_copy(a):
            part = pl.ds(a * depth, depth)
            source = records_hbm.at[pl.ds(step * step_rows, step_rows), part]
            return pltpu.make_async_copy(source, traces.at[:, part], trace_sem.at[a])

        def table_copy(a):
            part = pl.ds(a * depth, depth)
            return pltpu.make_async_copy(table_hbm.at[part], table.at[part], table_sem.at[a])

        for a in range(DEPTH_CHUNKS):
            trace_copy(a).start()
            pl.when(step == 0)(table_copy(a).start)
        both = jnp.zeros((step_rows, 4 * BINS), jnp.float32)
        for a in range(DEPTH_CHUNKS):
            trace_copy(a).wait()
            pl.when(step == 0)(table_copy(a).wait)
            part = slice(a * depth, (a + 1) * depth)
            both += jnp.dot(traces[:, part], table[part], preferred_element_type=jnp.float32)
        spectrum = both[:, : 2 * BINS] + both[:, 2 * BINS :]
        for block in range(step_blocks):
            part = spectrum[block * BLOCK_CH : (block + 1) * BLOCK_CH]
            real, imag = part[:, :BINS], part[:, BINS:]
            level = jnp.mean(real * real + imag * imag, axis=0, keepdims=True)
            scale = 1.0 / jnp.sqrt(level + 1e-05)
            for index, value in enumerate((real * scale, imag * scale)):
                rounded = value.astype(jnp.bfloat16)
                held[block, 0, index] = rounded[:HALF_CH]
                held[block, 1, index] = rounded[HALF_CH:]
            mine_ref[step * step_blocks + block] = held[block, half]
            other_ref[step * step_blocks + block] = held[block, 1 - half]

    shape = (blocks, 2, HALF_CH, BINS)
    return pl.pallas_call(
        kernel,
        grid=(blocks // step_blocks,),
        in_specs=[pl.BlockSpec(memory_space=pl.ANY)] * 2,
        out_specs=[VMEM_SPEC] * 2,
        out_shape=[pltpu.VMEM(shape, jnp.bfloat16)] * 2,
        scratch_shapes=[
            pltpu.VMEM((step_blocks, 2, 2, HALF_CH, BINS), jnp.bfloat16),
            pltpu.VMEM((step_rows, SAMPLES), jnp.bfloat16),
            pltpu.VMEM((SAMPLES, 4 * BINS), jnp.bfloat16),
            pltpu.SemaphoreType.DMA((DEPTH_CHUNKS,)),
            pltpu.SemaphoreType.DMA((DEPTH_CHUNKS,)),
        ],
        name="whiten",
    )(records, jnp.asarray(fourier_table()))


def group_is_window(group, offset_total):
    return group <= 16 and offset_total == 2


def slot_total(group, offset_total):
    return 2 if group_is_window(group, offset_total) else 2 * offset_total


def slot_pair(row, slot, offset_at, group, offset_total):
    if group_is_window(group, offset_total):
        last = group - 1
        if slot == 0:
            ahead = row + offset_at(0)
            inside = ahead < group
            return jnp.where(inside, 0, 1), jnp.where(inside, 0, 1), jnp.where(inside, ahead, row - last)
        behind = row - offset_at(0)
        inside = behind >= 0
        return jnp.where(inside, 1, 0), jnp.where(inside, 0, 1), jnp.where(inside, behind, row + last)
    side, k = slot // offset_total, slot % offset_total
    return side, k, row - offset_at(k) if side else row + offset_at(k)


def in_vmem(value):
    return pltpu.with_memory_space_constraint(value, pltpu.VMEM)


def pack(pieces, offsets, source_side, group, turns):
    offset_total = offsets.shape[0]
    slots = slot_total(group, offset_total)
    piece_blocks = pieces[0].shape[0]
    rows = (1 + slots) * SLOT_ROWS

    def kernel(offsets_ref, side_ref, *refs):
        piece_refs, out_refs, held = refs[: len(pieces)], refs[len(pieces) : -1], refs[-1]
        own_row, pair = lax.axis_index("blk"), lax.axis_index("pair")
        for turn, piece_ref in enumerate(piece_refs):
            first = (pair ^ turn) * piece_blocks
            for block in range(piece_blocks):
                held[first + block] = piece_ref[block].reshape(SLOT_ROWS, BINS)
        lane = lax.broadcasted_iota(jnp.int32, (FLAG_ROWS, BINS), 1)
        flags = jnp.zeros((FLAG_ROWS, BINS), jnp.float32)
        for k in range(offset_total):
            flags = jnp.where(lane == k, side_ref[0, k].astype(jnp.float32), flags)
        flags = flags.astype(jnp.bfloat16)

        def fill(row, out_ref):
            out_ref[:SLOT_ROWS] = held[row]
            for slot in range(slots):
                _, _, partner = slot_pair(row, slot, lambda k: offsets_ref[k], group, offset_total)
                partner = jnp.clip(partner, 0, group - 1)
                out_ref[(slot + 1) * SLOT_ROWS : (slot + 2) * SLOT_ROWS] = held[partner]
            out_ref[rows:] = flags

        if turns:
            for turn, out_ref in zip(turns, out_refs):
                fill(own_row ^ turn, out_ref)
        else:

            @pl.loop(0, group)
            def _(row):
                fill(row, out_refs[0].at[row])

    shape = (rows + FLAG_ROWS, BINS)
    if turns:
        out_shape = [pltpu.VMEM(shape, jnp.bfloat16)] * len(turns)
    else:
        out_shape = [jax.ShapeDtypeStruct((group,) + shape, jnp.bfloat16)]
    return pl.pallas_call(
        kernel,
        in_specs=[SMEM_SPEC, SMEM_SPEC] + [VMEM_SPEC] * len(pieces),
        out_specs=[VMEM_SPEC] * len(out_shape),
        out_shape=out_shape,
        scratch_shapes=[pltpu.VMEM((group, SLOT_ROWS, BINS), jnp.bfloat16)],
        name="pack",
    )(offsets, source_side, *[in_vmem(piece) for piece in pieces])


def correlate(mine, theirs, offsets, source_side, group, pairs, half_of, turns):
    offset_total = offsets.shape[0]
    slots = slot_total(group, offset_total)
    segs = len(turns) or mine.shape[0]
    chunk = len(turns) or SEGS_PER_STEP
    steps = segs // chunk
    lag_local = LAGS // pairs
    span = lag_local // 2
    left_rows, right_rows = (2 * span + 1) * BLOCK_CH, 2 * BLOCK_CH
    normalizer = 1.0 / math.sqrt(segs * BINS)
    flag_row = (1 + slots) * SLOT_ROWS
    count = len(turns) or 1

    def kernel(offsets_ref, side_ref, cos_mid, sin_mid, cos_away, sin_away, *refs):
        mine_refs, theirs_refs, refs = refs[:count], refs[count : 2 * count], refs[2 * count :]
        if turns:
            seg_refs = list(zip(mine_refs, theirs_refs))
        else:
            flags_ref, refs = refs[0], refs[1:]
            seg_refs = [(mine_refs[0].at[a], theirs_refs[0].at[a]) for a in range(chunk)]
        first_ref, second_ref, left, right, total = refs
        duo, step = pl.program_id(0), pl.program_id(1)
        row, pair = lax.axis_index("blk"), lax.axis_index("pair")
        half = half_of(pair)
        lane = lax.broadcasted_iota(jnp.int32, (FLAG_ROWS, BINS), 1)

        def far_side(other, k):
            if turns:
                flags = jnp.zeros((FLAG_ROWS, BINS), jnp.float32)
                for turn, (ref, _) in zip(turns, seg_refs):
                    piece = ref[flag_row:].astype(jnp.float32)
                    flags = jnp.where(row ^ turn == other, piece, flags)
            else:
                flags = flags_ref[other].astype(jnp.float32)
            return jnp.max(jnp.where(lane == k, flags, 0.0)) > 0.5

        lanes = []
        for a in range(2):
            side, k, other = 0, 0, 0
            for b in range(slots // 2):
                found = slot_pair(row, 2 * b + a, lambda j: offsets_ref[j], group, offset_total)
                side, k, other = [jnp.where(duo == b, x, y) for x, y in zip(found, (side, k, other))]
            valid = jnp.logical_and(other >= 0, other < group)
            far = far_side(jnp.clip(other, 0, group - 1), k)
            own_source = jnp.where(side == 0, side_ref[0, k] == 0, far)
            start = pl.multiple_of((2 * duo + a + 1) * SLOT_ROWS, SLOT_ROWS)
            lanes.append((side, k, valid, own_source, jnp.where(own_source, 1.0, -1.0), start))

        @pl.when(jnp.logical_and(duo == 0, step == 0))
        def _():
            first_ref[...] = jnp.zeros_like(first_ref)
            second_ref[...] = jnp.zeros_like(second_ref)

        @pl.when(jnp.logical_or(lanes[0][2], lanes[1][2]))
        def _():
            c_mid, s_mid = cos_mid[pl.ds(pair, 1)], sin_mid[pl.ds(pair, 1)]
            c_away, s_away = cos_away[...], sin_away[...]
            for seg, seg_pair in enumerate(seg_refs):
                for which, ref in zip((half, 1 - half), seg_pair):
                    top = pl.multiple_of(which * HALF_CH, HALF_CH)

                    def put(target, part, block, value):
                        rows = pl.ds(block * BLOCK_CH + top, HALF_CH)
                        target[2 * seg + part, rows] = value.astype(jnp.bfloat16)

                    real, imag = ref[:HALF_CH], ref[HALF_CH : 2 * HALF_CH]
                    put(left, 0, 0, real)
                    put(left, 1, 0, imag)
                    real, imag = real.astype(jnp.float32), imag.astype(jnp.float32)
                    for m in range(span):
                        c, s = c_away[m : m + 1], s_away[m : m + 1]
                        put(left, 0, 1 + m, real * c)
                        put(left, 1, 1 + m, imag * c)
                        put(left, 0, 1 + span + m, -(imag * s))
                        put(left, 1, 1 + span + m, real * s)
                    for a, (_, _, _, _, sign, start) in enumerate(lanes):
                        real = ref[pl.ds(start, HALF_CH)].astype(jnp.float32)
                        imag = ref[pl.ds(start + HALF_CH, HALF_CH)].astype(jnp.float32)
                        s = s_mid * sign
                        put(right, 0, a, real * c_mid - imag * s)
                        put(right, 1, a, imag * c_mid + real * s)
            product = lax.dot_general(
                jnp.concatenate([left[a] for a in range(2 * chunk)], axis=1),
                jnp.concatenate([right[a] for a in range(2 * chunk)], axis=1),
                (((1,), (1,)), ((), ())),
                preferred_element_type=jnp.float32,
            )
            if steps == 1:
                total[...] = product
            else:

                @pl.when(step == 0)
                def _():
                    total[...] = product

                @pl.when(step > 0)
                def _():
                    total[...] += product

        for a, (side, k, valid, own_source, sign, _) in enumerate(lanes):

            def emit(out_ref, turned):
                columns = slice(a * BLOCK_CH, (a + 1) * BLOCK_CH)
                for lag in range(lag_local):
                    m = abs(lag - span)
                    value = total[m * BLOCK_CH : (m + 1) * BLOCK_CH, columns]
                    if m:
                        at = (span + m) * BLOCK_CH
                        odd = total[at : at + BLOCK_CH, columns]
                        add = (lag < span) != turned
                        value = value + odd if add else value - odd
                    value = value * normalizer
                    out_ref[0, k, lag] = (value.T if turned else value).astype(jnp.bfloat16)

            for a_side, out_ref in enumerate((first_ref, second_ref)):
                for turned in (False, True):
                    here = jnp.logical_and(valid, step == steps - 1)
                    here = jnp.logical_and(here, side == a_side)
                    here = jnp.logical_and(here, own_source != turned)

                    @pl.when(here)
                    def _():
                        emit(out_ref, turned)

    out_shape = (1, offset_total, lag_local, BLOCK_CH, BLOCK_CH)
    out_spec = pl.BlockSpec(out_shape, lambda a, b: (0, 0, 0, 0, 0))
    if turns:
        operands = [in_vmem(piece) for piece in mine + theirs]
        specs = [VMEM_SPEC] * len(operands)
    else:
        flag_block = flag_row // FLAG_ROWS
        piece = pl.BlockSpec((chunk,) + mine.shape[1:], lambda a, b: (b, 0, 0))
        operands = [mine, theirs, mine]
        specs = [piece, piece, pl.BlockSpec((segs, FLAG_ROWS, BINS), lambda a, b: (0, flag_block, 0))]
    return pl.pallas_call(
        kernel,
        grid=(slots // 2, steps),
        in_specs=[SMEM_SPEC, SMEM_SPEC] + [VMEM_SPEC] * 4 + specs,
        out_specs=[out_spec] * 2,
        out_shape=[jax.ShapeDtypeStruct(out_shape, jnp.bfloat16)] * 2,
        scratch_shapes=[
            pltpu.VMEM((2 * chunk, left_rows, BINS), jnp.bfloat16),
            pltpu.VMEM((2 * chunk, right_rows, BINS), jnp.bfloat16),
            pltpu.VMEM((left_rows, right_rows), jnp.float32),
        ],
        name="correlate",
    )(offsets, source_side, *lag_tables(pairs), *operands)


def local(records, offsets, source_side):
    group, pairs = lax.axis_size("blk"), lax.axis_size("pair")
    half_of = lambda pair: pair % 2
    assert records.shape[0] == 1

    def swap(value, axis, turn):
        return lax.ppermute(value, axis, [(a, a ^ turn) for a in range(lax.axis_size(axis))])

    mine, other = whiten(records.reshape(records.shape[1], SAMPLES), half_of)
    pieces = [mine] + [swap(other if turn % 2 else mine, "pair", turn) for turn in range(1, pairs)]
    turns = TURNS if group == len(TURNS) else ()
    packed = pack(pieces, offsets, source_side, group, turns)
    if turns:
        arrived = [swap(value, "blk", turn) if turn else value for turn, value in zip(turns, packed)]
        arrived_other = [swap(value, "pair", 1) for value in arrived]
    else:
        arrived = lax.all_to_all(packed[0], "blk", split_axis=0, concat_axis=0, tiled=True)
        arrived_other = swap(arrived, "pair", 1)
    return correlate(arrived, arrived_other, offsets, source_side, group, pairs, half_of, turns)


def solution(mesh):
    placed = (P("blk", "pair", None), P(), P("blk", None))
    return jax.shard_map(
        local,
        mesh=mesh,
        in_specs=placed,
        out_specs=(P("blk", None, "pair", None, None), P("blk", None, "pair", None, None)),
        check_vma=False,
    )
```

```python
import math

import jax
import jax.numpy as jnp
import numpy as np
from jax import lax
from jax.experimental import pallas as pl
from jax.experimental.pallas import tpu as pltpu
from jax.sharding import PartitionSpec as P


BLOCK_CH = 128
BINS = 128
SAMPLES = 2048
FIRST_BIN = 4
LAGS = 32
HALF_CH = BLOCK_CH // 2
BLOCKS_PER_STEP = 2
DEPTH_CHUNKS = 4
TURNS = ((0, 2), (4, 4), (5, 4), (6, 2), (7, 2), (2, 2), (3, 2), (1, 2))
SEGS_PER_STEP = 8
FLAG_ROWS = 8
SMEM_SPEC = pl.BlockSpec(memory_space=pltpu.SMEM)
VMEM_SPEC = pl.BlockSpec(memory_space=pltpu.VMEM)


def fourier_table():
    sample_index = np.arange(SAMPLES)
    bin_index = FIRST_BIN + np.arange(BINS)
    angles = 2.0 * math.pi / SAMPLES * (sample_index[:, None] * bin_index[None, :] % SAMPLES)
    hann_taper = 0.5 - 0.5 * np.cos(2.0 * math.pi / SAMPLES * sample_index)
    full = np.concatenate(
        (hann_taper[:, None] * np.cos(angles), -hann_taper[:, None] * np.sin(angles)), axis=1
    ).astype(np.float32)
    high = full.astype(jnp.bfloat16)
    low = (full - high.astype(np.float32)).astype(jnp.bfloat16)
    return np.concatenate((high, low), axis=1)


def lag_tables(pairs):
    theta = 2.0 * math.pi / SAMPLES * (FIRST_BIN + np.arange(BINS))
    lag_local = LAGS // pairs
    middle = np.arange(pairs) * lag_local + lag_local // 2 - LAGS // 2
    away = np.arange(1, lag_local // 2 + 1)
    tables = [f(lags[:, None] * theta[None]) for lags in (middle, away) for f in (np.cos, np.sin)]
    return [jnp.asarray(table.astype(np.float32)) for table in tables]


def whiten(records, half_of):
    blocks = records.shape[0] // BLOCK_CH
    step_blocks = min(BLOCKS_PER_STEP, blocks)
    step_rows = step_blocks * BLOCK_CH
    depth = SAMPLES // DEPTH_CHUNKS

    def kernel(records_hbm, table_hbm, mine_ref, other_ref, held, traces, table, trace_sem, table_sem):
        step = pl.program_id(0)
        half = half_of(lax.axis_index("pair"))

        def trace_copy(a):
            part = pl.ds(a * depth, depth)
            source = records_hbm.at[pl.ds(step * step_rows, step_rows), part]
            return pltpu.make_async_copy(source, traces.at[:, part], trace_sem.at[a])

        def table_copy(a):
            part = pl.ds(a * depth, depth)
            return pltpu.make_async_copy(table_hbm.at[part], table.at[part], table_sem.at[a])

        for a in range(DEPTH_CHUNKS):
            trace_copy(a).start()
            pl.when(step == 0)(table_copy(a).start)
        both = jnp.zeros((step_rows, 4 * BINS), jnp.float32)
        for a in range(DEPTH_CHUNKS):
            trace_copy(a).wait()
            pl.when(step == 0)(table_copy(a).wait)
            part = slice(a * depth, (a + 1) * depth)
            both += jnp.dot(traces[:, part], table[part], preferred_element_type=jnp.float32)
        spectrum = both[:, : 2 * BINS] + both[:, 2 * BINS :]
        for block in range(step_blocks):
            part = spectrum[block * BLOCK_CH : (block + 1) * BLOCK_CH]
            real, imag = part[:, :BINS], part[:, BINS:]
            level = jnp.mean(real * real + imag * imag, axis=0, keepdims=True)
            scale = 1.0 / jnp.sqrt(level + 1e-05)
            for index, value in enumerate((real * scale, imag * scale)):
                rounded = value.astype(jnp.bfloat16)
                held[block, 0, index] = rounded[:HALF_CH]
                held[block, 1, index] = rounded[HALF_CH:]
            mine_ref[step * step_blocks + block] = held[block, half]
            other_ref[step * step_blocks + block] = held[block, 1 - half]

    shape = (blocks, 2, HALF_CH, BINS)
    return pl.pallas_call(
        kernel,
        grid=(blocks // step_blocks,),
        in_specs=[pl.BlockSpec(memory_space=pl.ANY)] * 2,
        out_specs=[VMEM_SPEC] * 2,
        out_shape=[pltpu.VMEM(shape, jnp.bfloat16)] * 2,
        scratch_shapes=[
            pltpu.VMEM((step_blocks, 2, 2, HALF_CH, BINS), jnp.bfloat16),
            pltpu.VMEM((step_rows, SAMPLES), jnp.bfloat16),
            pltpu.VMEM((SAMPLES, 4 * BINS), jnp.bfloat16),
            pltpu.SemaphoreType.DMA((DEPTH_CHUNKS,)),
            pltpu.SemaphoreType.DMA((DEPTH_CHUNKS,)),
        ],
        name="whiten",
    )(records, jnp.asarray(fourier_table()))


def group_is_window(group, offset_total):
    return group <= 16 and offset_total == 2


def slot_total(group, offset_total):
    return 2 if group_is_window(group, offset_total) else 2 * offset_total


def slot_pair(row, slot, offset_at, group, offset_total):
    if group_is_window(group, offset_total):
        last = group - 1
        if slot == 0:
            ahead = row + offset_at(0)
            inside = ahead < group
            return jnp.where(inside, 0, 1), jnp.where(inside, 0, 1), jnp.where(inside, ahead, row - last)
        behind = row - offset_at(0)
        inside = behind >= 0
        return jnp.where(inside, 1, 0), jnp.where(inside, 0, 1), jnp.where(inside, behind, row + last)
    side, k = slot // offset_total, slot % offset_total
    return side, k, row - offset_at(k) if side else row + offset_at(k)


def in_vmem(value):
    return pltpu.with_memory_space_constraint(value, pltpu.VMEM)


def part_top(pair, parts):
    top = pair % 2 * HALF_CH
    return top if parts == 2 else top + pair // 2 % 2 * (HALF_CH // 2)


def flag_at(slots, parts):
    return (1 + slots) * 2 * (BLOCK_CH // parts)


def pack(pieces, offsets, source_side, group, turns):
    offset_total = offsets.shape[0]
    slots = slot_total(group, offset_total)
    piece_blocks = pieces[0].shape[0]

    def kernel(offsets_ref, side_ref, *refs):
        piece_refs, out_refs, held = refs[: len(pieces)], refs[len(pieces) : -1], refs[-1]
        own_row, pair = lax.axis_index("blk"), lax.axis_index("pair")
        for turn, piece_ref in enumerate(piece_refs):
            first = (pair ^ turn) * piece_blocks
            for block in range(piece_blocks):
                held[first + block] = piece_ref[block]
        lane = lax.broadcasted_iota(jnp.int32, (FLAG_ROWS, BINS), 1)
        flags = jnp.zeros((FLAG_ROWS, BINS), jnp.float32)
        for k in range(offset_total):
            flags = jnp.where(lane == k, side_ref[0, k].astype(jnp.float32), flags)
        flags = flags.astype(jnp.bfloat16)

        def fill(row, out_ref, parts):
            count = BLOCK_CH // parts
            top = pl.multiple_of(part_top(pair, parts) - part_top(pair, 2), count)
            blocks = [row]
            for slot in range(slots):
                _, _, partner = slot_pair(row, slot, lambda k: offsets_ref[k], group, offset_total)
                blocks.append(jnp.clip(partner, 0, group - 1))
            for index, block in enumerate(blocks):
                for part in range(2):
                    at = (2 * index + part) * count
                    out_ref[at : at + count] = held[block, part, pl.ds(top, count)]
            out_ref[flag_at(slots, parts) :] = flags

        if turns:
            for (turn, parts), out_ref in zip(turns, out_refs):
                fill(own_row ^ turn, out_ref, parts)
        else:

            @pl.loop(0, group)
            def _(row):
                fill(row, out_refs[0].at[row], 2)

    def shape(parts):
        return (flag_at(slots, parts) + FLAG_ROWS, BINS)

    if turns:
        out_shape = [pltpu.VMEM(shape(parts), jnp.bfloat16) for _, parts in turns]
    else:
        out_shape = [jax.ShapeDtypeStruct((group,) + shape(2), jnp.bfloat16)]
    return pl.pallas_call(
        kernel,
        in_specs=[SMEM_SPEC, SMEM_SPEC] + [VMEM_SPEC] * len(pieces),
        out_specs=[VMEM_SPEC] * len(out_shape),
        out_shape=out_shape,
        scratch_shapes=[pltpu.VMEM((group, 2, HALF_CH, BINS), jnp.bfloat16)],
        name="pack",
    )(offsets, source_side, *[in_vmem(piece) for piece in pieces])


def describe_slots(row, duo, offsets_ref, side_ref, far_side, group, offset_total):
    found = []
    for a in range(2):
        side, k, other = 0, 0, 0
        for b in range(slot_total(group, offset_total) // 2):
            here = slot_pair(row, 2 * b + a, lambda j: offsets_ref[j], group, offset_total)
            side, k, other = [jnp.where(duo == b, x, y) for x, y in zip(here, (side, k, other))]
        valid = jnp.logical_and(other >= 0, other < group)
        far = far_side(jnp.clip(other, 0, group - 1), k)
        own_source = jnp.where(side == 0, side_ref[0, k] == 0, far)
        found.append((side, k, valid, own_source))
    return found


def fill_factors(segments, slot_list, duo, pair, tables, left, right):
    cos_mid, sin_mid, cos_away, sin_away = tables
    span = cos_away.shape[0]
    c_mid, s_mid = cos_mid[pl.ds(pair, 1)], sin_mid[pl.ds(pair, 1)]
    c_away, s_away = cos_away[...], sin_away[...]
    for seg, parts in enumerate(segments):
        count = BLOCK_CH // len(parts)
        for turn, ref in enumerate(parts):
            top = pl.multiple_of(part_top(pair ^ turn, len(parts)), count)

            def put(target, part, block, value):
                rows = pl.ds(block * BLOCK_CH + top, count)
                target[2 * seg + part, rows] = value.astype(jnp.bfloat16)

            real, imag = ref[:count], ref[count : 2 * count]
            put(left, 0, 0, real)
            put(left, 1, 0, imag)
            real, imag = real.astype(jnp.float32), imag.astype(jnp.float32)
            for m in range(span):
                c, s = c_away[m : m + 1], s_away[m : m + 1]
                put(left, 0, 1 + m, real * c)
                put(left, 1, 1 + m, imag * c)
                put(left, 0, 1 + span + m, -(imag * s))
                put(left, 1, 1 + span + m, real * s)
            for a, (_, _, _, own_source) in enumerate(slot_list):
                start = pl.multiple_of((2 * duo + a + 1) * 2 * count, 2 * count)
                real = ref[pl.ds(start, count)].astype(jnp.float32)
                imag = ref[pl.ds(start + count, count)].astype(jnp.float32)
                s = s_mid * jnp.where(own_source, 1.0, -1.0)
                put(right, 0, a, real * c_mid - imag * s)
                put(right, 1, a, imag * c_mid + real * s)


def contract(left, right):
    wide = lambda ref: jnp.concatenate([ref[a] for a in range(ref.shape[0])], axis=1)
    return lax.dot_general(
        wide(left), wide(right), (((1,), (1,)), ((), ())), preferred_element_type=jnp.float32
    )


def lag_values(totals, a, span, normalizer, turned, put):
    columns = slice(a * BLOCK_CH, (a + 1) * BLOCK_CH)

    def rows(at):
        found = [total[at * BLOCK_CH : (at + 1) * BLOCK_CH, columns] for total in totals]
        return sum(found[1:], found[0])

    even, odd = [rows(m) for m in range(span + 1)], [None] + [rows(span + m) for m in range(1, span + 1)]
    for lag in range(2 * span):
        m = abs(lag - span)
        value = even[m]
        if m:
            value = value + odd[m] if (lag < span) != turned else value - odd[m]
        value = value * normalizer
        put(lag, (value.T if turned else value).astype(jnp.bfloat16))


def factor_scratch(segs, span):
    return [
        pltpu.VMEM((2 * segs, (2 * span + 1) * BLOCK_CH, BINS), jnp.bfloat16),
        pltpu.VMEM((2 * segs, 2 * BLOCK_CH, BINS), jnp.bfloat16),
    ]


def correlate_all(mine, theirs, offsets, source_side, group, pairs):
    offset_total = offsets.shape[0]
    slots = slot_total(group, offset_total)
    segs = mine.shape[0]
    steps = segs // SEGS_PER_STEP
    lag_local = LAGS // pairs
    span = lag_local // 2
    normalizer = 1.0 / math.sqrt(segs * BINS)
    total_shape = ((2 * span + 1) * BLOCK_CH, 2 * BLOCK_CH)

    def kernel(offsets_ref, side_ref, *refs):
        tables, (mine_ref, theirs_ref, flags_ref, first_ref, second_ref, left, right, total) = refs[:4], refs[4:]
        duo, step = pl.program_id(0), pl.program_id(1)
        row, pair = lax.axis_index("blk"), lax.axis_index("pair")
        lane = lax.broadcasted_iota(jnp.int32, (FLAG_ROWS, BINS), 1)

        def far_side(other, k):
            return jnp.max(jnp.where(lane == k, flags_ref[other].astype(jnp.float32), 0.0)) > 0.5

        found = describe_slots(row, duo, offsets_ref, side_ref, far_side, group, offset_total)

        @pl.when(jnp.logical_and(duo == 0, step == 0))
        def _():
            first_ref[...] = jnp.zeros_like(first_ref)
            second_ref[...] = jnp.zeros_like(second_ref)

        segments = [(mine_ref.at[a], theirs_ref.at[a]) for a in range(SEGS_PER_STEP)]
        fill_factors(segments, found, duo, pair, tables, left, right)
        product = contract(left, right)

        @pl.when(step == 0)
        def _():
            total[...] = product

        @pl.when(step > 0)
        def _():
            total[...] += product

        for a, (side, k, valid, own_source) in enumerate(found):
            for a_side, out_ref in enumerate((first_ref, second_ref)):
                for turned in (False, True):
                    here = jnp.logical_and(valid, step == steps - 1)
                    here = jnp.logical_and(here, side == a_side)
                    here = jnp.logical_and(here, own_source != turned)

                    @pl.when(here)
                    def _():
                        def put(lag, value):
                            out_ref[0, k, lag] = value

                        lag_values([total], a, span, normalizer, turned, put)

    out_shape = (1, offset_total, lag_local, BLOCK_CH, BLOCK_CH)
    out_spec = pl.BlockSpec(out_shape, lambda a, b: (0, 0, 0, 0, 0))
    flag_block = flag_at(slots, 2) // FLAG_ROWS
    piece = pl.BlockSpec((SEGS_PER_STEP,) + mine.shape[1:], lambda a, b: (b, 0, 0))
    flags = pl.BlockSpec((segs, FLAG_ROWS, BINS), lambda a, b: (0, flag_block, 0))
    return pl.pallas_call(
        kernel,
        grid=(slots // 2, steps),
        in_specs=[SMEM_SPEC, SMEM_SPEC] + [VMEM_SPEC] * 4 + [piece, piece, flags],
        out_specs=[out_spec] * 2,
        out_shape=[jax.ShapeDtypeStruct(out_shape, jnp.bfloat16)] * 2,
        scratch_shapes=factor_scratch(SEGS_PER_STEP, span) + [pltpu.VMEM(total_shape, jnp.float32)],
        name="correlate",
    )(offsets, source_side, *lag_tables(pairs), mine, theirs, mine)


def zero_outputs(after, shape):
    def kernel(after_ref, first_hbm, second_hbm, zeros, sems):
        zeros[...] = jnp.zeros_like(zeros)
        copies = [
            pltpu.make_async_copy(zeros, ref.at[0, k], sems.at[side, k])
            for side, ref in enumerate((first_hbm, second_hbm))
            for k in range(shape[1])
        ]
        for copy in copies:
            copy.start()
        for copy in copies:
            copy.wait()

    any_spec = pl.BlockSpec(memory_space=pl.ANY)
    return pl.pallas_call(
        kernel,
        in_specs=[VMEM_SPEC],
        out_specs=[any_spec] * 2,
        out_shape=[jax.ShapeDtypeStruct(shape, jnp.bfloat16)] * 2,
        scratch_shapes=[
            pltpu.VMEM(shape[2:], jnp.bfloat16),
            pltpu.SemaphoreType.DMA((2, shape[1])),
        ],
        name="zeros",
    )(in_vmem(after))


def correlate_turns(turns, segments, empty, offsets, source_side, group, pairs):
    offset_total = offsets.shape[0]
    slots = slot_total(group, offset_total)
    lag_local = LAGS // pairs
    span = lag_local // 2
    normalizer = 1.0 / math.sqrt(len(turns) * BINS)
    total_shape = ((2 * span + 1) * BLOCK_CH, 2 * BLOCK_CH)
    counts = [len(parts) for parts in segments]

    def kernel(offsets_ref, side_ref, *refs):
        tables, refs = refs[:4], refs[4:]
        held = []
        for count in counts:
            held.append(refs[:count])
            refs = refs[count:]
        _, _, first_hbm, second_hbm, left, right, total, result, sems = refs
        row, pair = lax.axis_index("blk"), lax.axis_index("pair")
        lane = lax.broadcasted_iota(jnp.int32, (FLAG_ROWS, BINS), 1)

        def far_side(other, k):
            flags = jnp.zeros((FLAG_ROWS, BINS), jnp.float32)
            for (turn, _), parts in zip(turns, held):
                piece = parts[0][flag_at(slots, len(parts)) :].astype(jnp.float32)
                flags = jnp.where(row ^ turn == other, piece, flags)
            return jnp.max(jnp.where(lane == k, flags, 0.0)) > 0.5

        found = describe_slots(row, 0, offsets_ref, side_ref, far_side, group, offset_total)

        def copy_to(out_hbm, a, k, lag):
            return pltpu.make_async_copy(result.at[a, lag], out_hbm.at[0, k, lag], sems.at[a, lag])

        @pl.when(jnp.logical_or(found[0][2], found[1][2]))
        def _():
            fill_factors(held, found, 0, pair, tables, left, right)
            total[...] = contract(left, right)

        for a, (side, k, valid, own_source) in enumerate(found):
            for turned in (False, True):

                @pl.when(jnp.logical_and(valid, own_source != turned))
                def _():
                    def put(lag, value):
                        result[a, lag] = value
                        pl.when(side == 0)(copy_to(first_hbm, a, k, lag).start)
                        pl.when(side != 0)(copy_to(second_hbm, a, k, lag).start)

                    lag_values([total], a, span, normalizer, turned, put)

        for a, (side, k, valid, own_source) in enumerate(found):

            @pl.when(valid)
            def _():
                for lag in range(lag_local):
                    copy_to(first_hbm, a, 0, lag).wait()

    any_spec = pl.BlockSpec(memory_space=pl.ANY)
    operands = [in_vmem(part) for parts in segments for part in parts]
    aliased = 6 + len(operands)
    return pl.pallas_call(
        kernel,
        in_specs=[SMEM_SPEC, SMEM_SPEC] + [VMEM_SPEC] * (4 + len(operands)) + [any_spec] * 2,
        out_specs=[any_spec] * 2,
        out_shape=[jax.ShapeDtypeStruct(part.shape, part.dtype) for part in empty],
        input_output_aliases={aliased: 0, aliased + 1: 1},
        scratch_shapes=factor_scratch(len(turns), span)
        + [
            pltpu.VMEM(total_shape, jnp.float32),
            pltpu.VMEM((2, lag_local, BLOCK_CH, BLOCK_CH), jnp.bfloat16),
            pltpu.SemaphoreType.DMA((2, lag_local)),
        ],
        name="correlate",
    )(offsets, source_side, *lag_tables(pairs), *operands, *empty)


def local(records, offsets, source_side):
    group, pairs = lax.axis_size("blk"), lax.axis_size("pair")
    half_of = lambda pair: pair % 2
    assert records.shape[0] == 1

    def swap(value, axis, turn):
        return lax.ppermute(value, axis, [(a, a ^ turn) for a in range(lax.axis_size(axis))])

    mine, other = whiten(records.reshape(records.shape[1], SAMPLES), half_of)
    pieces = [mine]
    for turn in range(1, pairs):
        pieces.append(swap(other if turn % 2 else mine, "pair", turn))
    turns = turns_of(group, pairs)
    packed = pack(pieces, offsets, source_side, group, turns)
    if not turns:
        arrived = lax.all_to_all(packed[0], "blk", split_axis=0, concat_axis=0, tiled=True)
        theirs = swap(arrived, "pair", 1)
        return correlate_all(arrived, theirs, offsets, source_side, group, pairs)
    segments = []
    for (turn, parts), value in zip(turns, packed):
        arrived = swap(value, "blk", turn) if turn else value
        hops = [swap(arrived, "pair", hop) for hop in range(1, parts)]
        segments.append([arrived] + hops)
    shape = (1, offsets.shape[0], LAGS // pairs, BLOCK_CH, BLOCK_CH)
    empty = zero_outputs(segments[0][1], shape)
    return correlate_turns(turns, segments, empty, offsets, source_side, group, pairs)


def turns_of(group, pairs):
    return TURNS if group == len(TURNS) and pairs == 4 else ()


def solution(mesh):
    placed = (P("blk", "pair", None), P(), P("blk", None))

    return jax.shard_map(
        local,
        mesh=mesh,
        in_specs=placed,
        out_specs=(P("blk", None, "pair", None, None), P("blk", None, "pair", None, None)),
        check_vma=False,
    )
```

```python
import math

import jax
import jax.numpy as jnp
import numpy as np
from jax import lax
from jax.experimental import pallas as pl
from jax.experimental.pallas import tpu as pltpu
from jax.sharding import PartitionSpec as P


BLOCK_CH = 128
BINS = 128
SAMPLES = 2048
FIRST_BIN = 4
LAGS = 32
HALF_CH = BLOCK_CH // 2
BLOCKS_PER_STEP = 2
DEPTH_CHUNKS = 4
TURNS = ((0, 2), (6, 4), (4, 4), (1, 2), (3, 2), (5, 2), (7, 2), (2, 2))
SEGS_PER_STEP = 8
FLAG_ROWS = 8
SMEM_SPEC = pl.BlockSpec(memory_space=pltpu.SMEM)
VMEM_SPEC = pl.BlockSpec(memory_space=pltpu.VMEM)


def fourier_table():
    sample_index = np.arange(SAMPLES)
    bin_index = FIRST_BIN + np.arange(BINS)
    angles = 2.0 * math.pi / SAMPLES * (sample_index[:, None] * bin_index[None, :] % SAMPLES)
    hann_taper = 0.5 - 0.5 * np.cos(2.0 * math.pi / SAMPLES * sample_index)
    full = np.concatenate(
        (hann_taper[:, None] * np.cos(angles), -hann_taper[:, None] * np.sin(angles)), axis=1
    ).astype(np.float32)
    high = full.astype(jnp.bfloat16)
    low = (full - high.astype(np.float32)).astype(jnp.bfloat16)
    return np.concatenate((high, low), axis=1)


def lag_tables(pairs):
    theta = 2.0 * math.pi / SAMPLES * (FIRST_BIN + np.arange(BINS))
    lag_local = LAGS // pairs
    middle = np.arange(pairs) * lag_local + 0.5 * (lag_local - 1) - LAGS // 2
    away = (np.arange(lag_local // 2) + 0.5)[:, None] * theta
    middle = middle[:, None] * theta
    tables = np.cos(middle), np.sin(middle), np.stack((np.cos(away), np.sin(away), -np.sin(away)))
    return [jnp.asarray(table.astype(np.float32)) for table in tables]


def whiten(records, half_of):
    blocks = records.shape[0] // BLOCK_CH
    step_blocks = min(BLOCKS_PER_STEP, blocks)
    step_rows = step_blocks * BLOCK_CH
    depth = SAMPLES // DEPTH_CHUNKS

    def kernel(records_hbm, table_hbm, mine_ref, other_ref, held, traces, table, trace_sem, table_sem):
        step = pl.program_id(0)
        half = half_of(lax.axis_index("pair"))

        def trace_copy(a):
            part = pl.ds(a * depth, depth)
            source = records_hbm.at[pl.ds(step * step_rows, step_rows), part]
            return pltpu.make_async_copy(source, traces.at[:, part], trace_sem.at[a])

        def table_copy(a):
            part = pl.ds(a * depth, depth)
            return pltpu.make_async_copy(table_hbm.at[part], table.at[part], table_sem.at[a])

        for a in range(DEPTH_CHUNKS):
            trace_copy(a).start()
            pl.when(step == 0)(table_copy(a).start)
        both = jnp.zeros((step_rows, 4 * BINS), jnp.float32)
        for a in range(DEPTH_CHUNKS):
            trace_copy(a).wait()
            pl.when(step == 0)(table_copy(a).wait)
            part = slice(a * depth, (a + 1) * depth)
            both += jnp.dot(traces[:, part], table[part], preferred_element_type=jnp.float32)
        spectrum = both[:, : 2 * BINS] + both[:, 2 * BINS :]
        for block in range(step_blocks):
            part = spectrum[block * BLOCK_CH : (block + 1) * BLOCK_CH]
            real, imag = part[:, :BINS], part[:, BINS:]
            level = jnp.mean(real * real + imag * imag, axis=0, keepdims=True)
            scale = 1.0 / jnp.sqrt(level + 1e-05)
            for index, value in enumerate((real * scale, imag * scale)):
                rounded = value.astype(jnp.bfloat16)
                held[block, 0, index] = rounded[:HALF_CH]
                held[block, 1, index] = rounded[HALF_CH:]
            mine_ref[step * step_blocks + block] = held[block, half]
            other_ref[step * step_blocks + block] = held[block, 1 - half]

    shape = (blocks, 2, HALF_CH, BINS)
    return pl.pallas_call(
        kernel,
        grid=(blocks // step_blocks,),
        in_specs=[pl.BlockSpec(memory_space=pl.ANY)] * 2,
        out_specs=[VMEM_SPEC] * 2,
        out_shape=[pltpu.VMEM(shape, jnp.bfloat16)] * 2,
        scratch_shapes=[
            pltpu.VMEM((step_blocks, 2, 2, HALF_CH, BINS), jnp.bfloat16),
            pltpu.VMEM((step_rows, SAMPLES), jnp.bfloat16),
            pltpu.VMEM((SAMPLES, 4 * BINS), jnp.bfloat16),
            pltpu.SemaphoreType.DMA((DEPTH_CHUNKS,)),
            pltpu.SemaphoreType.DMA((DEPTH_CHUNKS,)),
        ],
        name="whiten",
    )(records, jnp.asarray(fourier_table()))


def group_is_window(group, offset_total):
    return group <= 16 and offset_total == 2


def slot_total(group, offset_total):
    return 2 if group_is_window(group, offset_total) else 2 * offset_total


def slot_pair(row, slot, offset_at, group, offset_total):
    if group_is_window(group, offset_total):
        last = group - 1
        if slot == 0:
            ahead = row + offset_at(0)
            inside = ahead < group
            return jnp.where(inside, 0, 1), jnp.where(inside, 0, 1), jnp.where(inside, ahead, row - last)
        behind = row - offset_at(0)
        inside = behind >= 0
        return jnp.where(inside, 1, 0), jnp.where(inside, 0, 1), jnp.where(inside, behind, row + last)
    side, k = slot // offset_total, slot % offset_total
    return side, k, row - offset_at(k) if side else row + offset_at(k)


def in_vmem(value):
    return pltpu.with_memory_space_constraint(value, pltpu.VMEM)


def part_top(pair, parts):
    top = pair % 2 * HALF_CH
    return top if parts == 2 else top + pair // 2 % 2 * (HALF_CH // 2)


def flag_at(slots, parts):
    return (1 + slots) * 2 * (BLOCK_CH // parts)


def pack(pieces, offsets, source_side, group, turns):
    offset_total = offsets.shape[0]
    slots = slot_total(group, offset_total)
    piece_blocks = pieces[0].shape[0]

    def kernel(offsets_ref, side_ref, *refs):
        piece_refs, out_refs, held = refs[: len(pieces)], refs[len(pieces) : -1], refs[-1]
        own_row, pair = lax.axis_index("blk"), lax.axis_index("pair")
        for turn, piece_ref in enumerate(piece_refs):
            first = (pair ^ turn) * piece_blocks
            for block in range(piece_blocks):
                held[first + block] = piece_ref[block]
        lane = lax.broadcasted_iota(jnp.int32, (FLAG_ROWS, BINS), 1)
        flags = jnp.zeros((FLAG_ROWS, BINS), jnp.float32)
        for k in range(offset_total):
            flags = jnp.where(lane == k, side_ref[0, k].astype(jnp.float32), flags)
        flags = flags.astype(jnp.bfloat16)

        def fill(row, out_ref, parts):
            count = BLOCK_CH // parts
            top = pl.multiple_of(part_top(pair, parts) - part_top(pair, 2), count)
            blocks = [row]
            for slot in range(slots):
                _, _, partner = slot_pair(row, slot, lambda k: offsets_ref[k], group, offset_total)
                blocks.append(jnp.clip(partner, 0, group - 1))
            for index, block in enumerate(blocks):
                for part in range(2):
                    at = (2 * index + part) * count
                    out_ref[at : at + count] = held[block, part, pl.ds(top, count)]
            out_ref[flag_at(slots, parts) :] = flags

        if turns:
            for (turn, parts), out_ref in zip(turns, out_refs):
                fill(own_row ^ turn, out_ref, parts)
        else:

            @pl.loop(0, group)
            def _(row):
                fill(row, out_refs[0].at[row], 2)

    def shape(parts):
        return (flag_at(slots, parts) + FLAG_ROWS, BINS)

    if turns:
        out_shape = [pltpu.VMEM(shape(parts), jnp.bfloat16) for _, parts in turns]
    else:
        out_shape = [jax.ShapeDtypeStruct((group,) + shape(2), jnp.bfloat16)]
    return pl.pallas_call(
        kernel,
        in_specs=[SMEM_SPEC, SMEM_SPEC] + [VMEM_SPEC] * len(pieces),
        out_specs=[VMEM_SPEC] * len(out_shape),
        out_shape=out_shape,
        scratch_shapes=[pltpu.VMEM((group, 2, HALF_CH, BINS), jnp.bfloat16)],
        name="pack",
    )(offsets, source_side, *[in_vmem(piece) for piece in pieces])


def describe_slots(row, duo, offsets_ref, side_ref, far_side, group, offset_total):
    found = []
    for a in range(2):
        side, k, other = 0, 0, 0
        for b in range(slot_total(group, offset_total) // 2):
            here = slot_pair(row, 2 * b + a, lambda j: offsets_ref[j], group, offset_total)
            side, k, other = [jnp.where(duo == b, x, y) for x, y in zip(here, (side, k, other))]
        valid = jnp.logical_and(other >= 0, other < group)
        far = far_side(jnp.clip(other, 0, group - 1), k)
        own_source = jnp.where(side == 0, side_ref[0, k] == 0, far)
        found.append((side, k, valid, own_source))
    return found


def fill_factors(segments, slot_list, duo, pair, tables, left, right):
    cos_mid, sin_mid, away = tables
    span = away.shape[1]
    c_mid, s_mid = cos_mid[pl.ds(pair, 1)], sin_mid[pl.ds(pair, 1)]
    for seg, parts in enumerate(segments):
        count = BLOCK_CH // len(parts)
        for turn, ref in enumerate(parts):
            top = pl.multiple_of(part_top(pair ^ turn, len(parts)), count)

            def put(target, part, block, value):
                rows = pl.ds(block * BLOCK_CH + top, count)
                target[2 * seg + part, rows] = value.astype(jnp.bfloat16)

            real, imag = ref[:count].astype(jnp.float32), ref[count : 2 * count].astype(jnp.float32)
            for m in range(span):
                c, s, minus = [away[a, m : m + 1] for a in range(3)]
                put(left, 0, m, real * c)
                put(left, 1, m, imag * c)
                put(left, 0, span + m, imag * minus)
                put(left, 1, span + m, real * s)
            for a, (_, _, _, own_source) in enumerate(slot_list):
                start = pl.multiple_of((2 * duo + a + 1) * 2 * count, 2 * count)
                real = ref[pl.ds(start, count)].astype(jnp.float32)
                imag = ref[pl.ds(start + count, count)].astype(jnp.float32)
                s = s_mid * jnp.where(own_source, 1.0, -1.0)
                put(right, 0, a, real * c_mid - imag * s)
                put(right, 1, a, imag * c_mid + real * s)


def contract(left, right):
    wide = lambda ref: jnp.concatenate([ref[a] for a in range(ref.shape[0])], axis=1)
    return lax.dot_general(
        wide(left), wide(right), (((1,), (1,)), ((), ())), preferred_element_type=jnp.float32
    )


def lag_values(totals, a, span, normalizer, turned, put):
    columns = slice(a * BLOCK_CH, (a + 1) * BLOCK_CH)

    def rows(at):
        found = [total[at * BLOCK_CH : (at + 1) * BLOCK_CH, columns] for total in totals]
        return sum(found[1:], found[0]) * normalizer

    for m in range(span):
        even, odd = rows(m), rows(span + m)
        for lag, plus in ((span - 1 - m, not turned), (span + m, turned)):
            value = even + odd if plus else even - odd
            put(lag, (value.T if turned else value).astype(jnp.bfloat16))


def factor_scratch(segs, span):
    return [
        pltpu.VMEM((2 * segs, 2 * span * BLOCK_CH, BINS), jnp.bfloat16),
        pltpu.VMEM((2 * segs, 2 * BLOCK_CH, BINS), jnp.bfloat16),
    ]


def correlate_all(mine, theirs, offsets, source_side, group, pairs):
    offset_total = offsets.shape[0]
    slots = slot_total(group, offset_total)
    segs = mine.shape[0]
    steps = segs // SEGS_PER_STEP
    lag_local = LAGS // pairs
    span = lag_local // 2
    normalizer = 1.0 / math.sqrt(segs * BINS)
    total_shape = (2 * span * BLOCK_CH, 2 * BLOCK_CH)

    def kernel(offsets_ref, side_ref, *refs):
        tables, (mine_ref, theirs_ref, flags_ref, first_ref, second_ref, left, right, total) = refs[:3], refs[3:]
        duo, step = pl.program_id(0), pl.program_id(1)
        row, pair = lax.axis_index("blk"), lax.axis_index("pair")
        lane = lax.broadcasted_iota(jnp.int32, (FLAG_ROWS, BINS), 1)

        def far_side(other, k):
            return jnp.max(jnp.where(lane == k, flags_ref[other].astype(jnp.float32), 0.0)) > 0.5

        found = describe_slots(row, duo, offsets_ref, side_ref, far_side, group, offset_total)

        @pl.when(jnp.logical_and(duo == 0, step == 0))
        def _():
            first_ref[...] = jnp.zeros_like(first_ref)
            second_ref[...] = jnp.zeros_like(second_ref)

        segments = [(mine_ref.at[a], theirs_ref.at[a]) for a in range(SEGS_PER_STEP)]
        fill_factors(segments, found, duo, pair, tables, left, right)
        product = contract(left, right)

        @pl.when(step == 0)
        def _():
            total[...] = product

        @pl.when(step > 0)
        def _():
            total[...] += product

        for a, (side, k, valid, own_source) in enumerate(found):
            for a_side, out_ref in enumerate((first_ref, second_ref)):
                for turned in (False, True):
                    here = jnp.logical_and(valid, step == steps - 1)
                    here = jnp.logical_and(here, side == a_side)
                    here = jnp.logical_and(here, own_source != turned)

                    @pl.when(here)
                    def _():
                        def put(lag, value):
                            out_ref[0, k, lag] = value

                        lag_values([total], a, span, normalizer, turned, put)

    out_shape = (1, offset_total, lag_local, BLOCK_CH, BLOCK_CH)
    out_spec = pl.BlockSpec(out_shape, lambda a, b: (0, 0, 0, 0, 0))
    flag_block = flag_at(slots, 2) // FLAG_ROWS
    piece = pl.BlockSpec((SEGS_PER_STEP,) + mine.shape[1:], lambda a, b: (b, 0, 0))
    flags = pl.BlockSpec((segs, FLAG_ROWS, BINS), lambda a, b: (0, flag_block, 0))
    return pl.pallas_call(
        kernel,
        grid=(slots // 2, steps),
        in_specs=[SMEM_SPEC, SMEM_SPEC] + [VMEM_SPEC] * 3 + [piece, piece, flags],
        out_specs=[out_spec] * 2,
        out_shape=[jax.ShapeDtypeStruct(out_shape, jnp.bfloat16)] * 2,
        scratch_shapes=factor_scratch(SEGS_PER_STEP, span) + [pltpu.VMEM(total_shape, jnp.float32)],
        name="correlate",
    )(offsets, source_side, *lag_tables(pairs), mine, theirs, mine)


def correlate_turns(turns, segments, offsets, source_side, group, pairs):
    offset_total = offsets.shape[0]
    slots = slot_total(group, offset_total)
    lag_local = LAGS // pairs
    span = lag_local // 2
    normalizer = 1.0 / math.sqrt(len(turns) * BINS)
    total_shape = (2 * span * BLOCK_CH, 2 * BLOCK_CH)
    out_shape = (1, offset_total, lag_local, BLOCK_CH, BLOCK_CH)
    counts = [len(parts) for parts in segments]

    def kernel(offsets_ref, side_ref, *refs):
        tables, refs = refs[:3], refs[3:]
        held = []
        for count in counts:
            held.append(refs[:count])
            refs = refs[count:]
        first_hbm, second_hbm, left, right, total, result, zeros, sems, zero_sems = refs
        row, pair = lax.axis_index("blk"), lax.axis_index("pair")
        lane = lax.broadcasted_iota(jnp.int32, (FLAG_ROWS, BINS), 1)

        def far_side(other, k):
            flags = jnp.zeros((FLAG_ROWS, BINS), jnp.float32)
            for (turn, _), parts in zip(turns, held):
                piece = parts[0][flag_at(slots, len(parts)) :].astype(jnp.float32)
                flags = jnp.where(row ^ turn == other, piece, flags)
            return jnp.max(jnp.where(lane == k, flags, 0.0)) > 0.5

        found = describe_slots(row, 0, offsets_ref, side_ref, far_side, group, offset_total)

        slabs = []
        for side, out_hbm in enumerate((first_hbm, second_hbm)):
            for k in range(offset_total):
                pair_row = row - offsets_ref[k] if side else row + offsets_ref[k]
                is_pair = jnp.logical_and(pair_row >= 0, pair_row < group)
                copy = pltpu.make_async_copy(zeros, out_hbm.at[0, k], zero_sems.at[side, k])
                slabs.append((jnp.logical_not(is_pair), copy))
        zeros[...] = jnp.zeros_like(zeros)
        for blank, copy in slabs:
            pl.when(blank)(copy.start)

        def copy_to(out_hbm, a, k, lag):
            return pltpu.make_async_copy(result.at[a, lag], out_hbm.at[0, k, lag], sems.at[a, lag])

        @pl.when(jnp.logical_or(found[0][2], found[1][2]))
        def _():
            fill_factors(held, found, 0, pair, tables, left, right)
            total[...] = contract(left, right)

        for a, (side, k, valid, own_source) in enumerate(found):
            for turned in (False, True):

                @pl.when(jnp.logical_and(valid, own_source != turned))
                def _():
                    def put(lag, value):
                        result[a, lag] = value
                        pl.when(side == 0)(copy_to(first_hbm, a, k, lag).start)
                        pl.when(side != 0)(copy_to(second_hbm, a, k, lag).start)

                    lag_values([total], a, span, normalizer, turned, put)

        for a, (side, k, valid, own_source) in enumerate(found):

            @pl.when(valid)
            def _():
                for lag in range(lag_local):
                    copy_to(first_hbm, a, 0, lag).wait()

        for blank, copy in slabs:
            pl.when(blank)(copy.wait)

    any_spec = pl.BlockSpec(memory_space=pl.ANY)
    operands = [in_vmem(part) for parts in segments for part in parts]
    return pl.pallas_call(
        kernel,
        in_specs=[SMEM_SPEC, SMEM_SPEC] + [VMEM_SPEC] * (3 + len(operands)),
        out_specs=[any_spec] * 2,
        out_shape=[jax.ShapeDtypeStruct(out_shape, jnp.bfloat16)] * 2,
        scratch_shapes=factor_scratch(len(turns), span)
        + [
            pltpu.VMEM(total_shape, jnp.float32),
            pltpu.VMEM((2, lag_local, BLOCK_CH, BLOCK_CH), jnp.bfloat16),
            pltpu.VMEM((lag_local, BLOCK_CH, BLOCK_CH), jnp.bfloat16),
            pltpu.SemaphoreType.DMA((2, lag_local)),
            pltpu.SemaphoreType.DMA((2, offset_total)),
        ],
        name="correlate",
    )(offsets, source_side, *lag_tables(pairs), *operands)


def local(records, offsets, source_side):
    group, pairs = lax.axis_size("blk"), lax.axis_size("pair")
    half_of = lambda pair: pair % 2
    assert records.shape[0] == 1

    def swap(value, axis, turn):
        return lax.ppermute(value, axis, [(a, a ^ turn) for a in range(lax.axis_size(axis))])

    mine, other = whiten(records.reshape(records.shape[1], SAMPLES), half_of)
    pieces = [mine]
    for turn in range(1, pairs):
        pieces.append(swap(other if turn % 2 else mine, "pair", turn))
    turns = turns_of(group, pairs)
    packed = pack(pieces, offsets, source_side, group, turns)
    if not turns:
        arrived = lax.all_to_all(packed[0], "blk", split_axis=0, concat_axis=0, tiled=True)
        theirs = swap(arrived, "pair", 1)
        return correlate_all(arrived, theirs, offsets, source_side, group, pairs)
    segments = []
    for (turn, parts), value in zip(turns, packed):
        arrived = swap(value, "blk", turn) if turn else value
        hops = [swap(arrived, "pair", hop) for hop in range(1, parts)]
        segments.append([arrived] + hops)
    return correlate_turns(turns, segments, offsets, source_side, group, pairs)


def turns_of(group, pairs):
    return TURNS if group == len(TURNS) and pairs == 4 else ()


def solution(mesh):
    placed = (P("blk", "pair", None), P(), P("blk", None))

    return jax.shard_map(
        local,
        mesh=mesh,
        in_specs=placed,
        out_specs=(P("blk", None, "pair", None, None), P("blk", None, "pair", None, None)),
        check_vma=False,
    )
```

```python
import math

import jax
import jax.numpy as jnp
import numpy as np
from jax import lax
from jax.experimental import pallas as pl
from jax.experimental.pallas import tpu as pltpu
from jax.sharding import PartitionSpec as P


BLOCK_CH = 128
BINS = 128
SAMPLES = 2048
FIRST_BIN = 4
LAGS = 32
HALF_CH = BLOCK_CH // 2
BLOCKS_PER_STEP = 2
DEPTH_CHUNKS = 2
TURNS = ((0, 2), (6, 4), (4, 4), (1, 2), (3, 2), (5, 2), (7, 2), (2, 2))
SEGS_PER_STEP = 8
FLAG_ROWS = 8
VMEM_SPEC = pl.BlockSpec(memory_space=pltpu.VMEM)


def fourier_table():
    sample_index = np.arange(SAMPLES)
    bin_index = FIRST_BIN + np.arange(BINS)
    angles = 2.0 * math.pi / SAMPLES * (sample_index[:, None] * bin_index[None, :] % SAMPLES)
    hann_taper = 0.5 - 0.5 * np.cos(2.0 * math.pi / SAMPLES * sample_index)
    full = np.concatenate(
        (hann_taper[:, None] * np.cos(angles), -hann_taper[:, None] * np.sin(angles)), axis=1
    ).astype(np.float32)
    high = full.astype(jnp.bfloat16)
    low = (full - high.astype(np.float32)).astype(jnp.bfloat16)
    return np.concatenate((high, low), axis=1)


def lag_tables(pairs, normalizer):
    theta = 2.0 * math.pi / SAMPLES * (FIRST_BIN + np.arange(BINS))
    lag_local = LAGS // pairs
    middle = np.arange(pairs) * lag_local + 0.5 * (lag_local - 1) - LAGS // 2
    away = (np.arange(lag_local // 2) + 0.5)[:, None] * theta
    middle = middle[:, None] * theta
    tables = normalizer * np.cos(middle), normalizer * np.sin(middle), np.stack((np.cos(away), np.sin(away), -np.sin(away)))
    return [jnp.asarray(table.astype(np.float32)) for table in tables]


def whiten(records, offsets, source_side, half_of):
    offset_total = offsets.shape[0]
    blocks = records.shape[0] // BLOCK_CH
    step_blocks = min(BLOCKS_PER_STEP, blocks)
    step_rows = step_blocks * BLOCK_CH
    depth = SAMPLES // DEPTH_CHUNKS

    def kernel(offsets_hbm, side_hbm, records_hbm, table_hbm, mine_ref, other_ref, info_ref, *scratch):
        held, traces, table, offsets_ref, side_ref, trace_sem, table_sem, small_sem = scratch
        step = pl.program_id(0)
        half = half_of(lax.axis_index("pair"))

        def trace_copy(a):
            part = pl.ds(a * depth, depth)
            source = records_hbm.at[pl.ds(step * step_rows, step_rows), part]
            return pltpu.make_async_copy(source, traces.at[:, part], trace_sem.at[a])

        def table_copy(a):
            part = pl.ds(a * depth, depth)
            return pltpu.make_async_copy(table_hbm.at[part], table.at[part], table_sem.at[a])

        for a in range(DEPTH_CHUNKS):
            trace_copy(a).start()
            pl.when(step == 0)(table_copy(a).start)
        small = (
            pltpu.make_async_copy(offsets_hbm, offsets_ref, small_sem.at[0]),
            pltpu.make_async_copy(side_hbm, side_ref, small_sem.at[1]),
        )
        for copy in small:
            copy.start()
        for copy in small:
            copy.wait()
        lane = lax.broadcasted_iota(jnp.int32, (FLAG_ROWS, BINS), 1)
        info = jnp.zeros((FLAG_ROWS, BINS), jnp.int32)
        for k in range(offset_total):
            info = jnp.where(lane == k, side_ref[0, k], info)
            info = jnp.where(lane == FLAG_ROWS + k, offsets_ref[k], info)
        info_ref[...] = info.astype(jnp.float32)
        both = jnp.zeros((step_rows, 4 * BINS), jnp.float32)
        for a in range(DEPTH_CHUNKS):
            trace_copy(a).wait()
            pl.when(step == 0)(table_copy(a).wait)
            part = slice(a * depth, (a + 1) * depth)
            both += jnp.dot(traces[:, part], table[part], preferred_element_type=jnp.float32)
        spectrum = both[:, : 2 * BINS] + both[:, 2 * BINS :]
        for block in range(step_blocks):
            part = spectrum[block * BLOCK_CH : (block + 1) * BLOCK_CH]
            real, imag = part[:, :BINS], part[:, BINS:]
            level = jnp.mean(real * real + imag * imag, axis=0, keepdims=True)
            scale = 1.0 / jnp.sqrt(level + 1e-05)
            for index, value in enumerate((real * scale, imag * scale)):
                rounded = value.astype(jnp.bfloat16)
                held[block, 0, index] = rounded[:HALF_CH]
                held[block, 1, index] = rounded[HALF_CH:]
            mine_ref[step * step_blocks + block] = held[block, half]
            other_ref[step * step_blocks + block] = held[block, 1 - half]

    shape = (blocks, 2, HALF_CH, BINS)
    return pl.pallas_call(
        kernel,
        grid=(blocks // step_blocks,),
        in_specs=[pl.BlockSpec(memory_space=pl.ANY)] * 4,
        out_specs=[VMEM_SPEC] * 3,
        out_shape=[pltpu.VMEM(shape, jnp.bfloat16)] * 2 + [pltpu.VMEM((FLAG_ROWS, BINS), jnp.float32)],
        scratch_shapes=[
            pltpu.VMEM((step_blocks, 2, 2, HALF_CH, BINS), jnp.bfloat16),
            pltpu.VMEM((step_rows, SAMPLES), jnp.bfloat16),
            pltpu.VMEM((SAMPLES, 4 * BINS), jnp.bfloat16),
            pltpu.SMEM(offsets.shape, jnp.int32),
            pltpu.SMEM(source_side.shape, jnp.int32),
            pltpu.SemaphoreType.DMA((DEPTH_CHUNKS,)),
            pltpu.SemaphoreType.DMA((DEPTH_CHUNKS,)),
            pltpu.SemaphoreType.DMA((2,)),
        ],
        name="whiten",
    )(offsets, source_side, records, jnp.asarray(fourier_table()))


def group_is_window(group, offset_total):
    return group <= 16 and offset_total == 2


def slot_total(group, offset_total):
    return 2 if group_is_window(group, offset_total) else 2 * offset_total


def slot_pair(row, slot, offset_at, group, offset_total):
    if group_is_window(group, offset_total):
        last = group - 1
        if slot == 0:
            ahead = row + offset_at(0)
            inside = ahead < group
            return jnp.where(inside, 0, 1), jnp.where(inside, 0, 1), jnp.where(inside, ahead, row - last)
        behind = row - offset_at(0)
        inside = behind >= 0
        return jnp.where(inside, 1, 0), jnp.where(inside, 0, 1), jnp.where(inside, behind, row + last)
    side, k = slot // offset_total, slot % offset_total
    return side, k, row - offset_at(k) if side else row + offset_at(k)


def in_vmem(value):
    return pltpu.with_memory_space_constraint(value, pltpu.VMEM)


def part_top(pair, parts):
    top = pair % 2 * HALF_CH
    return top if parts == 2 else top + pair // 2 % 2 * (HALF_CH // 2)


def flag_at(slots, parts):
    return (1 + slots) * 2 * (BLOCK_CH // parts)


def read_info(info_ref, offset_total):
    lane = lax.broadcasted_iota(jnp.int32, (FLAG_ROWS, BINS), 1)
    at = lambda index: jnp.max(jnp.where(lane == index, info_ref[...], 0.0)).astype(jnp.int32)
    return [at(FLAG_ROWS + k) for k in range(offset_total)], [at(k) for k in range(offset_total)]


def pack(pieces, info, offset_total, group, turns):
    slots = slot_total(group, offset_total)
    piece_blocks = pieces[0].shape[0]

    def kernel(info_ref, *refs):
        piece_refs, out_refs, held = refs[: len(pieces)], refs[len(pieces) : -1], refs[-1]
        own_row, pair = lax.axis_index("blk"), lax.axis_index("pair")
        for turn, piece_ref in enumerate(piece_refs):
            first = (pair ^ turn) * piece_blocks
            for block in range(piece_blocks):
                held[first + block] = piece_ref[block]
        offsets, _ = read_info(info_ref, offset_total)
        flags = info_ref[...].astype(jnp.bfloat16)

        def fill(row, out_ref, parts):
            count = BLOCK_CH // parts
            top = pl.multiple_of(part_top(pair, parts) - part_top(pair, 2), count)
            blocks = [row]
            for slot in range(slots):
                _, _, partner = slot_pair(row, slot, lambda k: offsets[k], group, offset_total)
                blocks.append(jnp.clip(partner, 0, group - 1))
            for index, block in enumerate(blocks):
                for part in range(2):
                    at = (2 * index + part) * count
                    out_ref[at : at + count] = held[block, part, pl.ds(top, count)]
            out_ref[flag_at(slots, parts) :] = flags

        if turns:
            for (turn, parts), out_ref in zip(turns, out_refs):
                fill(own_row ^ turn, out_ref, parts)
        else:

            @pl.loop(0, group)
            def _(row):
                fill(row, out_refs[0].at[row], 2)

    def shape(parts):
        return (flag_at(slots, parts) + FLAG_ROWS, BINS)

    if turns:
        out_shape = [pltpu.VMEM(shape(parts), jnp.bfloat16) for _, parts in turns]
    else:
        out_shape = [jax.ShapeDtypeStruct((group,) + shape(2), jnp.bfloat16)]
    return pl.pallas_call(
        kernel,
        in_specs=[VMEM_SPEC] * (1 + len(pieces)),
        out_specs=[VMEM_SPEC] * len(out_shape),
        out_shape=out_shape,
        scratch_shapes=[pltpu.VMEM((group, 2, HALF_CH, BINS), jnp.bfloat16)],
        name="pack",
    )(*[in_vmem(value) for value in [info, *pieces]])


def describe_slots(row, duo, offsets, sides, far_side, group, offset_total):
    found = []
    for a in range(2):
        side, k, other = 0, 0, 0
        for b in range(slot_total(group, offset_total) // 2):
            here = slot_pair(row, 2 * b + a, lambda j: offsets[j], group, offset_total)
            side, k, other = [jnp.where(duo == b, x, y) for x, y in zip(here, (side, k, other))]
        valid = jnp.logical_and(other >= 0, other < group)
        far = far_side(jnp.clip(other, 0, group - 1), k)
        own_side = sides[0]
        for j in range(1, offset_total):
            own_side = jnp.where(k == j, sides[j], own_side)
        own_source = jnp.where(side == 0, own_side == 0, far)
        found.append((side, k, valid, own_source))
    return found


def fill_factors(segments, slot_list, duo, pair, tables, left, right):
    cos_mid, sin_mid, away = tables
    span = away.shape[1]
    c_mid, s_mid = cos_mid[pl.ds(pair, 1)], sin_mid[pl.ds(pair, 1)]
    for seg, parts in enumerate(segments):
        count = BLOCK_CH // len(parts)
        for turn, ref in enumerate(parts):
            top = pl.multiple_of(part_top(pair ^ turn, len(parts)), count)

            def put(target, part, block, value):
                rows = pl.ds(block * BLOCK_CH + top, count)
                target[2 * seg + part, rows] = value.astype(jnp.bfloat16)

            real, imag = ref[:count].astype(jnp.float32), ref[count : 2 * count].astype(jnp.float32)
            for m in range(span):
                c, s, minus = [away[a, m : m + 1] for a in range(3)]
                put(left, 0, m, real * c)
                put(left, 1, m, imag * c)
                put(left, 0, span + m, imag * minus)
                put(left, 1, span + m, real * s)
            for a, (_, _, _, own_source) in enumerate(slot_list):
                start = pl.multiple_of((2 * duo + a + 1) * 2 * count, 2 * count)
                real = ref[pl.ds(start, count)].astype(jnp.float32)
                imag = ref[pl.ds(start + count, count)].astype(jnp.float32)
                s = s_mid * jnp.where(own_source, 1.0, -1.0)
                put(right, 0, a, real * c_mid - imag * s)
                put(right, 1, a, imag * c_mid + real * s)


def contract(left, right):
    wide = lambda ref: jnp.concatenate([ref[a] for a in range(ref.shape[0])], axis=1)
    return lax.dot_general(
        wide(left), wide(right), (((1,), (1,)), ((), ())), preferred_element_type=jnp.float32
    )


def lag_values(total, a, span, turned, put):
    columns = slice(a * BLOCK_CH, (a + 1) * BLOCK_CH)

    def rows(at):
        return total[at * BLOCK_CH : (at + 1) * BLOCK_CH, columns]

    for m in range(span):
        even, odd = rows(m), rows(span + m)
        for lag, plus in ((span - 1 - m, not turned), (span + m, turned)):
            value = even + odd if plus else even - odd
            put(lag, (value.T if turned else value).astype(jnp.bfloat16))


def factor_scratch(segs, span):
    return [
        pltpu.VMEM((2 * segs, 2 * span * BLOCK_CH, BINS), jnp.bfloat16),
        pltpu.VMEM((2 * segs, 2 * BLOCK_CH, BINS), jnp.bfloat16),
    ]


def correlate_all(mine, theirs, info, offset_total, group, pairs):
    slots = slot_total(group, offset_total)
    segs = mine.shape[0]
    steps = segs // SEGS_PER_STEP
    lag_local = LAGS // pairs
    span = lag_local // 2
    normalizer = 1.0 / math.sqrt(segs * BINS)
    total_shape = (2 * span * BLOCK_CH, 2 * BLOCK_CH)

    def kernel(info_ref, *refs):
        offsets, sides = read_info(info_ref, offset_total)
        tables, (mine_ref, theirs_ref, flags_ref, first_ref, second_ref, left, right, total) = refs[:3], refs[3:]
        duo, step = pl.program_id(0), pl.program_id(1)
        row, pair = lax.axis_index("blk"), lax.axis_index("pair")
        lane = lax.broadcasted_iota(jnp.int32, (FLAG_ROWS, BINS), 1)

        def far_side(other, k):
            return jnp.max(jnp.where(lane == k, flags_ref[other].astype(jnp.float32), 0.0)) > 0.5

        found = describe_slots(row, duo, offsets, sides, far_side, group, offset_total)

        @pl.when(jnp.logical_and(duo == 0, step == 0))
        def _():
            first_ref[...] = jnp.zeros_like(first_ref)
            second_ref[...] = jnp.zeros_like(second_ref)

        segments = [(mine_ref.at[a], theirs_ref.at[a]) for a in range(SEGS_PER_STEP)]
        fill_factors(segments, found, duo, pair, tables, left, right)
        product = contract(left, right)

        @pl.when(step == 0)
        def _():
            total[...] = product

        @pl.when(step > 0)
        def _():
            total[...] += product

        for a, (side, k, valid, own_source) in enumerate(found):
            for a_side, out_ref in enumerate((first_ref, second_ref)):
                for turned in (False, True):
                    here = jnp.logical_and(valid, step == steps - 1)
                    here = jnp.logical_and(here, side == a_side)
                    here = jnp.logical_and(here, own_source != turned)

                    @pl.when(here)
                    def _():
                        def put(lag, value):
                            out_ref[0, k, lag] = value

                        lag_values(total, a, span, turned, put)

    out_shape = (1, offset_total, lag_local, BLOCK_CH, BLOCK_CH)
    out_spec = pl.BlockSpec(out_shape, lambda a, b: (0, 0, 0, 0, 0))
    flag_block = flag_at(slots, 2) // FLAG_ROWS
    piece = pl.BlockSpec((SEGS_PER_STEP,) + mine.shape[1:], lambda a, b: (b, 0, 0))
    flags = pl.BlockSpec((segs, FLAG_ROWS, BINS), lambda a, b: (0, flag_block, 0))
    return pl.pallas_call(
        kernel,
        grid=(slots // 2, steps),
        in_specs=[VMEM_SPEC] * 4 + [piece, piece, flags],
        out_specs=[out_spec] * 2,
        out_shape=[jax.ShapeDtypeStruct(out_shape, jnp.bfloat16)] * 2,
        scratch_shapes=factor_scratch(SEGS_PER_STEP, span) + [pltpu.VMEM(total_shape, jnp.float32)],
        name="correlate",
    )(in_vmem(info), *lag_tables(pairs, normalizer), mine, theirs, mine)


def correlate_turns(turns, segments, info, offset_total, group, pairs):
    slots = slot_total(group, offset_total)
    lag_local = LAGS // pairs
    span = lag_local // 2
    normalizer = 1.0 / math.sqrt(len(turns) * BINS)
    total_shape = (2 * span * BLOCK_CH, 2 * BLOCK_CH)
    out_shape = (1, offset_total, lag_local, BLOCK_CH, BLOCK_CH)
    counts = [len(parts) for parts in segments]

    def kernel(info_ref, *refs):
        offsets, sides = read_info(info_ref, offset_total)
        tables, refs = refs[:3], refs[3:]
        held = []
        for count in counts:
            held.append(refs[:count])
            refs = refs[count:]
        first_hbm, second_hbm, left, right, total, result, zeros, sems, zero_sems = refs
        row, pair = lax.axis_index("blk"), lax.axis_index("pair")
        lane = lax.broadcasted_iota(jnp.int32, (FLAG_ROWS, BINS), 1)

        def far_side(other, k):
            flags = jnp.zeros((FLAG_ROWS, BINS), jnp.float32)
            for (turn, _), parts in zip(turns, held):
                piece = parts[0][flag_at(slots, len(parts)) :].astype(jnp.float32)
                flags = jnp.where(row ^ turn == other, piece, flags)
            return jnp.max(jnp.where(lane == k, flags, 0.0)) > 0.5

        found = describe_slots(row, 0, offsets, sides, far_side, group, offset_total)

        slabs = []
        for side, out_hbm in enumerate((first_hbm, second_hbm)):
            for k in range(offset_total):
                pair_row = row - offsets[k] if side else row + offsets[k]
                is_pair = jnp.logical_and(pair_row >= 0, pair_row < group)
                copy = pltpu.make_async_copy(zeros, out_hbm.at[0, k], zero_sems.at[side, k])
                slabs.append((jnp.logical_not(is_pair), copy))
        zeros[...] = jnp.zeros_like(zeros)
        for blank, copy in slabs:
            pl.when(blank)(copy.start)

        def copy_to(out_hbm, a, k, lag):
            return pltpu.make_async_copy(result.at[a, lag], out_hbm.at[0, k, lag], sems.at[a, lag])

        @pl.when(jnp.logical_or(found[0][2], found[1][2]))
        def _():
            fill_factors(held, found, 0, pair, tables, left, right)
            total[...] = contract(left, right)

        for a, (side, k, valid, own_source) in enumerate(found):
            for turned in (False, True):

                @pl.when(jnp.logical_and(valid, own_source != turned))
                def _():
                    def put(lag, value):
                        result[a, lag] = value
                        pl.when(side == 0)(copy_to(first_hbm, a, k, lag).start)
                        pl.when(side != 0)(copy_to(second_hbm, a, k, lag).start)

                    lag_values(total, a, span, turned, put)

        for a, (side, k, valid, own_source) in enumerate(found):

            @pl.when(valid)
            def _():
                for lag in range(lag_local):
                    copy_to(first_hbm, a, 0, lag).wait()

        for blank, copy in slabs:
            pl.when(blank)(copy.wait)

    any_spec = pl.BlockSpec(memory_space=pl.ANY)
    operands = [in_vmem(part) for parts in segments for part in parts]
    return pl.pallas_call(
        kernel,
        in_specs=[VMEM_SPEC] * (4 + len(operands)),
        out_specs=[any_spec] * 2,
        out_shape=[jax.ShapeDtypeStruct(out_shape, jnp.bfloat16)] * 2,
        scratch_shapes=factor_scratch(len(turns), span)
        + [
            pltpu.VMEM(total_shape, jnp.float32),
            pltpu.VMEM((2, lag_local, BLOCK_CH, BLOCK_CH), jnp.bfloat16),
            pltpu.VMEM((lag_local, BLOCK_CH, BLOCK_CH), jnp.bfloat16),
            pltpu.SemaphoreType.DMA((2, lag_local)),
            pltpu.SemaphoreType.DMA((2, offset_total)),
        ],
        name="correlate",
    )(*[in_vmem(value) for value in [info, *lag_tables(pairs, normalizer)]], *operands)


def local(records, offsets, source_side):
    group, pairs = lax.axis_size("blk"), lax.axis_size("pair")
    half_of = lambda pair: pair % 2
    assert records.shape[0] == 1

    def swap(value, axis, turn):
        return lax.ppermute(value, axis, [(a, a ^ turn) for a in range(lax.axis_size(axis))])

    offset_total = offsets.shape[0]
    traces = records.reshape(records.shape[1], SAMPLES)
    mine, other, info = whiten(traces, offsets, source_side, half_of)
    pieces = [mine]
    for turn in range(1, pairs):
        pieces.append(swap(other if turn % 2 else mine, "pair", turn))
    turns = turns_of(group, pairs)
    packed = pack(pieces, info, offset_total, group, turns)
    if not turns:
        arrived = lax.all_to_all(packed[0], "blk", split_axis=0, concat_axis=0, tiled=True)
        theirs = swap(arrived, "pair", 1)
        return correlate_all(arrived, theirs, info, offset_total, group, pairs)
    segments = []
    for (turn, parts), value in zip(turns, packed):
        arrived = swap(value, "blk", turn) if turn else value
        hops = [swap(arrived, "pair", hop) for hop in range(1, parts)]
        segments.append([arrived] + hops)
    return correlate_turns(turns, segments, info, offset_total, group, pairs)


def turns_of(group, pairs):
    return TURNS if group == len(TURNS) and pairs == 4 else ()


def solution(mesh):
    placed = (P("blk", "pair", None), P(), P("blk", None))

    return jax.shard_map(
        local,
        mesh=mesh,
        in_specs=placed,
        out_specs=(P("blk", None, "pair", None, None), P("blk", None, "pair", None, None)),
        check_vma=False,
    )
```

```python
import math

import jax
import jax.numpy as jnp
import numpy as np
from jax import lax
from jax.experimental import pallas as pl
from jax.experimental.pallas import tpu as pltpu
from jax.sharding import PartitionSpec as P


BLOCK_CH = 128
BINS = 128
SAMPLES = 2048
FIRST_BIN = 4
LAGS = 32
HALF_CH = BLOCK_CH // 2
BLOCKS_PER_STEP = 2
DEPTH_CHUNKS = 2
TURNS = ((0, 2), (6, 4), (4, 4), (1, 2), (3, 2), (5, 4), (7, 2), (2, 2))
JOINED = (0, 6, 4)
SEGS_PER_STEP = 8
FLAG_ROWS = 8
VMEM_SPEC = pl.BlockSpec(memory_space=pltpu.VMEM)


def fourier_table():
    sample_index = np.arange(SAMPLES)
    bin_index = FIRST_BIN + np.arange(BINS)
    angles = 2.0 * math.pi / SAMPLES * (sample_index[:, None] * bin_index[None, :] % SAMPLES)
    hann_taper = 0.5 - 0.5 * np.cos(2.0 * math.pi / SAMPLES * sample_index)
    full = np.concatenate(
        (hann_taper[:, None] * np.cos(angles), -hann_taper[:, None] * np.sin(angles)), axis=1
    ).astype(np.float32)
    high = full.astype(jnp.bfloat16)
    low = (full - high.astype(np.float32)).astype(jnp.bfloat16)
    return np.concatenate((high, low), axis=1)


def lag_tables(pairs, normalizer):
    theta = 2.0 * math.pi / SAMPLES * (FIRST_BIN + np.arange(BINS))
    lag_local = LAGS // pairs
    middle = np.arange(pairs) * lag_local + 0.5 * (lag_local - 1) - LAGS // 2
    away = (np.arange(lag_local // 2) + 0.5)[:, None] * theta
    middle = middle[:, None] * theta
    tables = normalizer * np.cos(middle), normalizer * np.sin(middle), np.stack((np.cos(away), np.sin(away), -np.sin(away)))
    return [jnp.asarray(table.astype(np.float32)) for table in tables]


def whiten(records, offsets, source_side, half_of):
    offset_total = offsets.shape[0]
    blocks = records.shape[0] // BLOCK_CH
    step_blocks = min(BLOCKS_PER_STEP, blocks)
    step_rows = step_blocks * BLOCK_CH
    depth = SAMPLES // DEPTH_CHUNKS

    def kernel(offsets_hbm, side_hbm, records_hbm, table_hbm, mine_ref, other_ref, info_ref, *scratch):
        held, traces, table, offsets_ref, side_ref, trace_sem, table_sem, small_sem = scratch
        step = pl.program_id(0)
        half = half_of(lax.axis_index("pair"))

        def trace_copy(a):
            part = pl.ds(a * depth, depth)
            source = records_hbm.at[pl.ds(step * step_rows, step_rows), part]
            return pltpu.make_async_copy(source, traces.at[:, part], trace_sem.at[a])

        def table_copy(a):
            part = pl.ds(a * depth, depth)
            return pltpu.make_async_copy(table_hbm.at[part], table.at[part], table_sem.at[a])

        for a in range(DEPTH_CHUNKS):
            trace_copy(a).start()
            pl.when(step == 0)(table_copy(a).start)
        small = (
            pltpu.make_async_copy(offsets_hbm, offsets_ref, small_sem.at[0]),
            pltpu.make_async_copy(side_hbm, side_ref, small_sem.at[1]),
        )
        for copy in small:
            copy.start()
        for copy in small:
            copy.wait()
        lane = lax.broadcasted_iota(jnp.int32, (FLAG_ROWS, BINS), 1)
        info = jnp.zeros((FLAG_ROWS, BINS), jnp.int32)
        for k in range(offset_total):
            info = jnp.where(lane == k, side_ref[0, k], info)
            info = jnp.where(lane == FLAG_ROWS + k, offsets_ref[k], info)
        info_ref[...] = info.astype(jnp.float32)
        both = jnp.zeros((step_rows, 4 * BINS), jnp.float32)
        for a in range(DEPTH_CHUNKS):
            trace_copy(a).wait()
            pl.when(step == 0)(table_copy(a).wait)
            part = slice(a * depth, (a + 1) * depth)
            both += jnp.dot(traces[:, part], table[part], preferred_element_type=jnp.float32)
        spectrum = both[:, : 2 * BINS] + both[:, 2 * BINS :]
        for block in range(step_blocks):
            part = spectrum[block * BLOCK_CH : (block + 1) * BLOCK_CH]
            real, imag = part[:, :BINS], part[:, BINS:]
            level = jnp.mean(real * real + imag * imag, axis=0, keepdims=True)
            scale = 1.0 / jnp.sqrt(level + 1e-05)
            for index, value in enumerate((real * scale, imag * scale)):
                rounded = value.astype(jnp.bfloat16)
                held[block, 0, index] = rounded[:HALF_CH]
                held[block, 1, index] = rounded[HALF_CH:]
            mine_ref[step * step_blocks + block] = held[block, half]
            other_ref[step * step_blocks + block] = held[block, 1 - half]

    shape = (blocks, 2, HALF_CH, BINS)
    return pl.pallas_call(
        kernel,
        grid=(blocks // step_blocks,),
        in_specs=[pl.BlockSpec(memory_space=pl.ANY)] * 4,
        out_specs=[VMEM_SPEC] * 3,
        out_shape=[pltpu.VMEM(shape, jnp.bfloat16)] * 2 + [pltpu.VMEM((FLAG_ROWS, BINS), jnp.float32)],
        scratch_shapes=[
            pltpu.VMEM((step_blocks, 2, 2, HALF_CH, BINS), jnp.bfloat16),
            pltpu.VMEM((step_rows, SAMPLES), jnp.bfloat16),
            pltpu.VMEM((SAMPLES, 4 * BINS), jnp.bfloat16),
            pltpu.SMEM(offsets.shape, jnp.int32),
            pltpu.SMEM(source_side.shape, jnp.int32),
            pltpu.SemaphoreType.DMA((DEPTH_CHUNKS,)),
            pltpu.SemaphoreType.DMA((DEPTH_CHUNKS,)),
            pltpu.SemaphoreType.DMA((2,)),
        ],
        name="whiten",
    )(offsets, source_side, records, jnp.asarray(fourier_table()))


def group_is_window(group, offset_total):
    return group <= 16 and offset_total == 2


def slot_total(group, offset_total):
    return 2 if group_is_window(group, offset_total) else 2 * offset_total


def slot_pair(row, slot, offset_at, group, offset_total):
    if group_is_window(group, offset_total):
        last = group - 1
        if slot == 0:
            ahead = row + offset_at(0)
            inside = ahead < group
            return jnp.where(inside, 0, 1), jnp.where(inside, 0, 1), jnp.where(inside, ahead, row - last)
        behind = row - offset_at(0)
        inside = behind >= 0
        return jnp.where(inside, 1, 0), jnp.where(inside, 0, 1), jnp.where(inside, behind, row + last)
    side, k = slot // offset_total, slot % offset_total
    return side, k, row - offset_at(k) if side else row + offset_at(k)


def in_vmem(value):
    return pltpu.with_memory_space_constraint(value, pltpu.VMEM)


def part_top(pair, parts):
    top = pair % 2 * HALF_CH
    return top if parts == 2 else top + pair // 2 % 2 * (HALF_CH // 2)


def flag_at(slots, parts):
    return (1 + slots) * 2 * (BLOCK_CH // parts)


def read_info(info_ref, offset_total):
    lane = lax.broadcasted_iota(jnp.int32, (FLAG_ROWS, BINS), 1)
    at = lambda index: jnp.max(jnp.where(lane == index, info_ref[...], 0.0)).astype(jnp.int32)
    return [at(FLAG_ROWS + k) for k in range(offset_total)], [at(k) for k in range(offset_total)]


def pack(pieces, info, offset_total, group, turns):
    slots = slot_total(group, offset_total)
    piece_blocks = pieces[0].shape[0]

    def kernel(info_ref, *refs):
        piece_refs, out_refs, held = refs[: len(pieces)], refs[len(pieces) : -1], refs[-1]
        own_row, pair = lax.axis_index("blk"), lax.axis_index("pair")
        for turn, piece_ref in enumerate(piece_refs):
            first = (pair ^ turn) * piece_blocks
            for block in range(piece_blocks):
                held[first + block] = piece_ref[block]
        offsets, _ = read_info(info_ref, offset_total)
        flags = info_ref[...].astype(jnp.bfloat16)

        def fill(row, out_ref, parts):
            count = BLOCK_CH // parts
            top = pl.multiple_of(part_top(pair, parts) - part_top(pair, 2), count)
            blocks = [row]
            for slot in range(slots):
                _, _, partner = slot_pair(row, slot, lambda k: offsets[k], group, offset_total)
                blocks.append(jnp.clip(partner, 0, group - 1))
            for index, block in enumerate(blocks):
                for part in range(2):
                    at = (2 * index + part) * count
                    out_ref[at : at + count] = held[block, part, pl.ds(top, count)]
            out_ref[flag_at(slots, parts) :] = flags

        if turns:
            for (turn, parts), out_ref in zip(turns, out_refs):
                fill(own_row ^ turn, out_ref, parts)
        else:

            @pl.loop(0, group)
            def _(row):
                fill(row, out_refs[0].at[row], 2)

    def shape(parts):
        return (flag_at(slots, parts) + FLAG_ROWS, BINS)

    if turns:
        out_shape = [pltpu.VMEM(shape(parts), jnp.bfloat16) for _, parts in turns]
    else:
        out_shape = [jax.ShapeDtypeStruct((group,) + shape(2), jnp.bfloat16)]
    return pl.pallas_call(
        kernel,
        in_specs=[VMEM_SPEC] * (1 + len(pieces)),
        out_specs=[VMEM_SPEC] * len(out_shape),
        out_shape=out_shape,
        scratch_shapes=[pltpu.VMEM((group, 2, HALF_CH, BINS), jnp.bfloat16)],
        name="pack",
    )(*[in_vmem(value) for value in [info, *pieces]])


def describe_slots(row, duo, offsets, sides, far_side, group, offset_total):
    found = []
    for a in range(2):
        side, k, other = 0, 0, 0
        for b in range(slot_total(group, offset_total) // 2):
            here = slot_pair(row, 2 * b + a, lambda j: offsets[j], group, offset_total)
            side, k, other = [jnp.where(duo == b, x, y) for x, y in zip(here, (side, k, other))]
        valid = jnp.logical_and(other >= 0, other < group)
        far = far_side(jnp.clip(other, 0, group - 1), k)
        own_side = sides[0]
        for j in range(1, offset_total):
            own_side = jnp.where(k == j, sides[j], own_side)
        own_source = jnp.where(side == 0, own_side == 0, far)
        found.append((side, k, valid, own_source))
    return found


def fill_factors(segments, slot_list, duo, pair, tables, left, right):
    cos_mid, sin_mid, away = tables
    span = away.shape[1]
    c_mid, s_mid = cos_mid[pl.ds(pair, 1)], sin_mid[pl.ds(pair, 1)]
    for seg, parts in enumerate(segments):
        count = BLOCK_CH // len(parts)
        for turn, ref in enumerate(parts):
            top = pl.multiple_of(part_top(pair ^ turn, len(parts)), count)

            def put(target, part, block, value):
                rows = pl.ds(block * BLOCK_CH + top, count)
                target[2 * seg + part, rows] = value.astype(jnp.bfloat16)

            real, imag = ref[:count].astype(jnp.float32), ref[count : 2 * count].astype(jnp.float32)
            for m in range(span):
                c, s, minus = [away[a, m : m + 1] for a in range(3)]
                put(left, 0, m, real * c)
                put(left, 1, m, imag * c)
                put(left, 0, span + m, imag * minus)
                put(left, 1, span + m, real * s)
            for a, (_, _, _, own_source) in enumerate(slot_list):
                start = pl.multiple_of((2 * duo + a + 1) * 2 * count, 2 * count)
                real = ref[pl.ds(start, count)].astype(jnp.float32)
                imag = ref[pl.ds(start + count, count)].astype(jnp.float32)
                s = s_mid * jnp.where(own_source, 1.0, -1.0)
                put(right, 0, a, real * c_mid - imag * s)
                put(right, 1, a, imag * c_mid + real * s)


def contract(left, right):
    wide = lambda ref: jnp.concatenate([ref[a] for a in range(ref.shape[0])], axis=1)
    return lax.dot_general(
        wide(left), wide(right), (((1,), (1,)), ((), ())), preferred_element_type=jnp.float32
    )


def lag_values(total, a, span, turned, put):
    columns = slice(a * BLOCK_CH, (a + 1) * BLOCK_CH)

    def rows(at):
        return total[at * BLOCK_CH : (at + 1) * BLOCK_CH, columns]

    for m in range(span):
        even, odd = rows(m), rows(span + m)
        for lag, plus in ((span - 1 - m, not turned), (span + m, turned)):
            value = even + odd if plus else even - odd
            put(lag, (value.T if turned else value).astype(jnp.bfloat16))


def factor_scratch(segs, span):
    return [
        pltpu.VMEM((2 * segs, 2 * span * BLOCK_CH, BINS), jnp.bfloat16),
        pltpu.VMEM((2 * segs, 2 * BLOCK_CH, BINS), jnp.bfloat16),
    ]


def correlate_all(mine, theirs, info, offset_total, group, pairs):
    slots = slot_total(group, offset_total)
    segs = mine.shape[0]
    steps = segs // SEGS_PER_STEP
    lag_local = LAGS // pairs
    span = lag_local // 2
    normalizer = 1.0 / math.sqrt(segs * BINS)
    total_shape = (2 * span * BLOCK_CH, 2 * BLOCK_CH)

    def kernel(info_ref, *refs):
        offsets, sides = read_info(info_ref, offset_total)
        tables, (mine_ref, theirs_ref, flags_ref, first_ref, second_ref, left, right, total) = refs[:3], refs[3:]
        duo, step = pl.program_id(0), pl.program_id(1)
        row, pair = lax.axis_index("blk"), lax.axis_index("pair")
        lane = lax.broadcasted_iota(jnp.int32, (FLAG_ROWS, BINS), 1)

        def far_side(other, k):
            return jnp.max(jnp.where(lane == k, flags_ref[other].astype(jnp.float32), 0.0)) > 0.5

        found = describe_slots(row, duo, offsets, sides, far_side, group, offset_total)

        @pl.when(jnp.logical_and(duo == 0, step == 0))
        def _():
            first_ref[...] = jnp.zeros_like(first_ref)
            second_ref[...] = jnp.zeros_like(second_ref)

        segments = [(mine_ref.at[a], theirs_ref.at[a]) for a in range(SEGS_PER_STEP)]
        fill_factors(segments, found, duo, pair, tables, left, right)
        product = contract(left, right)

        @pl.when(step == 0)
        def _():
            total[...] = product

        @pl.when(step > 0)
        def _():
            total[...] += product

        for a, (side, k, valid, own_source) in enumerate(found):
            for a_side, out_ref in enumerate((first_ref, second_ref)):
                for turned in (False, True):
                    here = jnp.logical_and(valid, step == steps - 1)
                    here = jnp.logical_and(here, side == a_side)
                    here = jnp.logical_and(here, own_source != turned)

                    @pl.when(here)
                    def _():
                        def put(lag, value):
                            out_ref[0, k, lag] = value

                        lag_values(total, a, span, turned, put)

    out_shape = (1, offset_total, lag_local, BLOCK_CH, BLOCK_CH)
    out_spec = pl.BlockSpec(out_shape, lambda a, b: (0, 0, 0, 0, 0))
    flag_block = flag_at(slots, 2) // FLAG_ROWS
    piece = pl.BlockSpec((SEGS_PER_STEP,) + mine.shape[1:], lambda a, b: (b, 0, 0))
    flags = pl.BlockSpec((segs, FLAG_ROWS, BINS), lambda a, b: (0, flag_block, 0))
    return pl.pallas_call(
        kernel,
        grid=(slots // 2, steps),
        in_specs=[VMEM_SPEC] * 4 + [piece, piece, flags],
        out_specs=[out_spec] * 2,
        out_shape=[jax.ShapeDtypeStruct(out_shape, jnp.bfloat16)] * 2,
        scratch_shapes=factor_scratch(SEGS_PER_STEP, span) + [pltpu.VMEM(total_shape, jnp.float32)],
        name="correlate",
    )(in_vmem(info), *lag_tables(pairs, normalizer), mine, theirs, mine)


def join(groups):
    arrays = [array for group in groups for array in group]
    counts = [len(group) for group in groups]

    def kernel(*refs):
        sources, targets = refs[: len(arrays)], refs[len(arrays) :]
        for count, target in zip(counts, targets):
            at = 0
            for source in sources[:count]:
                target[at : at + source.shape[0]] = source[...]
                at += source.shape[0]
            sources = sources[count:]

    out_shape = [
        pltpu.VMEM((sum(array.shape[0] for array in group), BINS), jnp.bfloat16) for group in groups
    ]
    return pl.pallas_call(
        kernel,
        in_specs=[VMEM_SPEC] * len(arrays),
        out_specs=[VMEM_SPEC] * len(groups),
        out_shape=out_shape,
        name="join",
    )(*[in_vmem(array) for array in arrays])


def correlate_turns(turns, segments, info, offset_total, group, pairs):
    slots = slot_total(group, offset_total)
    lag_local = LAGS // pairs
    span = lag_local // 2
    normalizer = 1.0 / math.sqrt(len(turns) * BINS)
    total_shape = (2 * span * BLOCK_CH, 2 * BLOCK_CH)
    out_shape = (1, offset_total, lag_local, BLOCK_CH, BLOCK_CH)
    arrays = []
    for parts in segments:
        arrays += [array for array, _ in parts if all(array is not other for other in arrays)]
    index_of = lambda array: [array is other for other in arrays].index(True)
    places = [[(index_of(array), at) for array, at in parts] for parts in segments]

    def kernel(info_ref, *refs):
        offsets, sides = read_info(info_ref, offset_total)
        tables, refs = refs[:3], refs[3:]
        held = []
        for parts in places:
            rows = flag_at(slots, len(parts)) + FLAG_ROWS
            held.append([refs[index].at[at : at + rows] for index, at in parts])
        refs = refs[len(arrays) :]
        first_hbm, second_hbm, left, right, total, result, zeros, sems, zero_sems = refs
        row, pair = lax.axis_index("blk"), lax.axis_index("pair")
        lane = lax.broadcasted_iota(jnp.int32, (FLAG_ROWS, BINS), 1)

        def far_side(other, k):
            flags = jnp.zeros((FLAG_ROWS, BINS), jnp.float32)
            for (turn, _), parts in zip(turns, held):
                piece = parts[0][flag_at(slots, len(parts)) :].astype(jnp.float32)
                flags = jnp.where(row ^ turn == other, piece, flags)
            return jnp.max(jnp.where(lane == k, flags, 0.0)) > 0.5

        found = describe_slots(row, 0, offsets, sides, far_side, group, offset_total)

        slabs = []
        for side, out_hbm in enumerate((first_hbm, second_hbm)):
            for k in range(offset_total):
                pair_row = row - offsets[k] if side else row + offsets[k]
                is_pair = jnp.logical_and(pair_row >= 0, pair_row < group)
                copy = pltpu.make_async_copy(zeros, out_hbm.at[0, k], zero_sems.at[side, k])
                slabs.append((jnp.logical_not(is_pair), copy))
        zeros[...] = jnp.zeros_like(zeros)
        for blank, copy in slabs:
            pl.when(blank)(copy.start)

        def copy_to(out_hbm, a, k, lag):
            return pltpu.make_async_copy(result.at[a, lag], out_hbm.at[0, k, lag], sems.at[a, lag])

        @pl.when(jnp.logical_or(found[0][2], found[1][2]))
        def _():
            fill_factors(held, found, 0, pair, tables, left, right)
            total[...] = contract(left, right)

        for a, (side, k, valid, own_source) in enumerate(found):
            for turned in (False, True):

                @pl.when(jnp.logical_and(valid, own_source != turned))
                def _():
                    def put(lag, value):
                        result[a, lag] = value
                        pl.when(side == 0)(copy_to(first_hbm, a, k, lag).start)
                        pl.when(side != 0)(copy_to(second_hbm, a, k, lag).start)

                    lag_values(total, a, span, turned, put)

        for a, (side, k, valid, own_source) in enumerate(found):

            @pl.when(valid)
            def _():
                for lag in range(lag_local):
                    copy_to(first_hbm, a, 0, lag).wait()

        for blank, copy in slabs:
            pl.when(blank)(copy.wait)

    any_spec = pl.BlockSpec(memory_space=pl.ANY)
    operands = [in_vmem(array) for array in arrays]
    return pl.pallas_call(
        kernel,
        in_specs=[VMEM_SPEC] * (4 + len(operands)),
        out_specs=[any_spec] * 2,
        out_shape=[jax.ShapeDtypeStruct(out_shape, jnp.bfloat16)] * 2,
        scratch_shapes=factor_scratch(len(turns), span)
        + [
            pltpu.VMEM(total_shape, jnp.float32),
            pltpu.VMEM((2, lag_local, BLOCK_CH, BLOCK_CH), jnp.bfloat16),
            pltpu.VMEM((lag_local, BLOCK_CH, BLOCK_CH), jnp.bfloat16),
            pltpu.SemaphoreType.DMA((2, lag_local)),
            pltpu.SemaphoreType.DMA((2, offset_total)),
        ],
        name="correlate",
    )(*[in_vmem(value) for value in [info, *lag_tables(pairs, normalizer)]], *operands)


def local(records, offsets, source_side):
    group, pairs = lax.axis_size("blk"), lax.axis_size("pair")
    half_of = lambda pair: pair % 2
    assert records.shape[0] == 1

    def swap(value, axis, turn):
        return lax.ppermute(value, axis, [(a, a ^ turn) for a in range(lax.axis_size(axis))])

    offset_total = offsets.shape[0]
    traces = records.reshape(records.shape[1], SAMPLES)
    mine, other, info = whiten(traces, offsets, source_side, half_of)
    pieces = [mine]
    for turn in range(1, pairs):
        pieces.append(swap(other if turn % 2 else mine, "pair", turn))
    turns = turns_of(group, pairs)
    packed = pack(pieces, info, offset_total, group, turns)
    if not turns:
        arrived = lax.all_to_all(packed[0], "blk", split_axis=0, concat_axis=0, tiled=True)
        theirs = swap(arrived, "pair", 1)
        return correlate_all(arrived, theirs, info, offset_total, group, pairs)
    parts_of = dict(turns)
    arrived = {}
    for (turn, _), value in zip(turns, packed):
        arrived[turn] = swap(value, "blk", turn) if turn else value
    quarters = [turn for turn in JOINED if parts_of[turn] == 4]
    below, both = join([[arrived[turn] for turn in quarters], [arrived[turn] for turn in JOINED]])
    below_2 = swap(below, "pair", 2)
    both_1 = swap(both, "pair", 1)
    below_3 = swap(below_2, "pair", 1)
    segments = []
    for turn, parts in turns:
        if turn in JOINED:
            ahead = JOINED[: JOINED.index(turn)]
            found = [(arrived[turn], 0), (both_1, sum(arrived[other].shape[0] for other in ahead))]
            if parts == 4:
                at = sum(arrived[other].shape[0] for other in ahead if other in quarters)
                found += [(below_2, at), (below_3, at)]
        else:
            hops = [swap(arrived[turn], "pair", hop) for hop in range(1, parts)]
            found = [(array, 0) for array in [arrived[turn]] + hops]
        segments.append(found)
    return correlate_turns(turns, segments, info, offset_total, group, pairs)


def turns_of(group, pairs):
    return TURNS if group == len(TURNS) and pairs == 4 else ()


def solution(mesh):
    placed = (P("blk", "pair", None), P(), P("blk", None))

    return jax.shard_map(
        local,
        mesh=mesh,
        in_specs=placed,
        out_specs=(P("blk", None, "pair", None, None), P("blk", None, "pair", None, None)),
        check_vma=False,
    )
```

```python
import math

import jax
import jax.numpy as jnp
import numpy as np
from jax import lax
from jax.experimental import pallas as pl
from jax.experimental.pallas import tpu as pltpu
from jax.sharding import PartitionSpec as P


BLOCK_CH = 128
BINS = 128
SAMPLES = 2048
FIRST_BIN = 4
LAGS = 32
HALF_CH = BLOCK_CH // 2
BLOCKS_PER_STEP = 2
DEPTH_CHUNKS = 2
TURNS = ((0, 2), (6, 4), (4, 4), (1, 2), (3, 2), (5, 4), (7, 2), (2, 2))
JOINED = (0, 6, 4)
SEGS_PER_STEP = 8
FLAG_ROWS = 8
VMEM_SPEC = pl.BlockSpec(memory_space=pltpu.VMEM)


def fourier_table():
    sample_index = np.arange(SAMPLES)
    bin_index = FIRST_BIN + np.arange(BINS)
    angles = 2.0 * math.pi / SAMPLES * (sample_index[:, None] * bin_index[None, :] % SAMPLES)
    hann_taper = 0.5 - 0.5 * np.cos(2.0 * math.pi / SAMPLES * sample_index)
    full = np.concatenate(
        (hann_taper[:, None] * np.cos(angles), -hann_taper[:, None] * np.sin(angles)), axis=1
    ).astype(np.float32)
    high = full.astype(jnp.bfloat16)
    low = (full - high.astype(np.float32)).astype(jnp.bfloat16)
    return np.concatenate((high, low), axis=1)


def lag_tables(pairs, normalizer):
    theta = 2.0 * math.pi / SAMPLES * (FIRST_BIN + np.arange(BINS))
    lag_local = LAGS // pairs
    middle = np.arange(pairs) * lag_local + 0.5 * (lag_local - 1) - LAGS // 2
    away = (np.arange(lag_local // 2) + 0.5)[:, None] * theta
    middle = middle[:, None] * theta
    tables = normalizer * np.cos(middle), normalizer * np.sin(middle), np.stack((np.cos(away), np.sin(away), -np.sin(away)))
    return [jnp.asarray(table.astype(np.float32)) for table in tables]


def whiten(records, offsets, source_side, half_of):
    offset_total = offsets.shape[0]
    blocks = records.shape[0] // BLOCK_CH
    step_blocks = min(BLOCKS_PER_STEP, blocks)
    step_rows = step_blocks * BLOCK_CH
    depth = SAMPLES // DEPTH_CHUNKS

    def kernel(offsets_hbm, side_hbm, records_hbm, table_hbm, mine_ref, other_ref, info_ref, *scratch):
        held, traces, table, offsets_ref, side_ref, trace_sem, table_sem, small_sem = scratch
        step = pl.program_id(0)
        half = half_of(lax.axis_index("pair"))

        def trace_copy(a):
            part = pl.ds(a * depth, depth)
            source = records_hbm.at[pl.ds(step * step_rows, step_rows), part]
            return pltpu.make_async_copy(source, traces.at[:, part], trace_sem.at[a])

        def table_copy(a):
            part = pl.ds(a * depth, depth)
            return pltpu.make_async_copy(table_hbm.at[part], table.at[part], table_sem.at[a])

        for a in range(DEPTH_CHUNKS):
            trace_copy(a).start()
            pl.when(step == 0)(table_copy(a).start)
        small = (
            pltpu.make_async_copy(offsets_hbm, offsets_ref, small_sem.at[0]),
            pltpu.make_async_copy(side_hbm, side_ref, small_sem.at[1]),
        )
        for copy in small:
            copy.start()
        for copy in small:
            copy.wait()
        lane = lax.broadcasted_iota(jnp.int32, (FLAG_ROWS, BINS), 1)
        info = jnp.zeros((FLAG_ROWS, BINS), jnp.int32)
        for k in range(offset_total):
            info = jnp.where(lane == k, side_ref[0, k], info)
            info = jnp.where(lane == FLAG_ROWS + k, offsets_ref[k], info)
        info_ref[...] = info.astype(jnp.float32)
        both = jnp.zeros((step_rows, 4 * BINS), jnp.float32)
        for a in range(DEPTH_CHUNKS):
            trace_copy(a).wait()
            pl.when(step == 0)(table_copy(a).wait)
            part = slice(a * depth, (a + 1) * depth)
            both += jnp.dot(traces[:, part], table[part], preferred_element_type=jnp.float32)
        spectrum = both[:, : 2 * BINS] + both[:, 2 * BINS :]
        for block in range(step_blocks):
            part = spectrum[block * BLOCK_CH : (block + 1) * BLOCK_CH]
            real, imag = part[:, :BINS], part[:, BINS:]
            level = jnp.mean(real * real + imag * imag, axis=0, keepdims=True)
            scale = 1.0 / jnp.sqrt(level + 1e-05)
            for index, value in enumerate((real * scale, imag * scale)):
                rounded = value.astype(jnp.bfloat16)
                held[block, 0, index] = rounded[:HALF_CH]
                held[block, 1, index] = rounded[HALF_CH:]
            mine_ref[step * step_blocks + block] = held[block, half]
            other_ref[step * step_blocks + block] = held[block, 1 - half]

    shape = (blocks, 2, HALF_CH, BINS)
    return pl.pallas_call(
        kernel,
        grid=(blocks // step_blocks,),
        in_specs=[pl.BlockSpec(memory_space=pl.ANY)] * 4,
        out_specs=[VMEM_SPEC] * 3,
        out_shape=[pltpu.VMEM(shape, jnp.bfloat16)] * 2 + [pltpu.VMEM((FLAG_ROWS, BINS), jnp.float32)],
        scratch_shapes=[
            pltpu.VMEM((step_blocks, 2, 2, HALF_CH, BINS), jnp.bfloat16),
            pltpu.VMEM((step_rows, SAMPLES), jnp.bfloat16),
            pltpu.VMEM((SAMPLES, 4 * BINS), jnp.bfloat16),
            pltpu.SMEM(offsets.shape, jnp.int32),
            pltpu.SMEM(source_side.shape, jnp.int32),
            pltpu.SemaphoreType.DMA((DEPTH_CHUNKS,)),
            pltpu.SemaphoreType.DMA((DEPTH_CHUNKS,)),
            pltpu.SemaphoreType.DMA((2,)),
        ],
        name="whiten",
    )(offsets, source_side, records, jnp.asarray(fourier_table()))


def group_is_window(group, offset_total):
    return group <= 16 and offset_total == 2


def slot_total(group, offset_total):
    return 2 if group_is_window(group, offset_total) else 2 * offset_total


def slot_pair(row, slot, offset_at, group, offset_total):
    if group_is_window(group, offset_total):
        last = group - 1
        if slot == 0:
            ahead = row + offset_at(0)
            inside = ahead < group
            return jnp.where(inside, 0, 1), jnp.where(inside, 0, 1), jnp.where(inside, ahead, row - last)
        behind = row - offset_at(0)
        inside = behind >= 0
        return jnp.where(inside, 1, 0), jnp.where(inside, 0, 1), jnp.where(inside, behind, row + last)
    side, k = slot // offset_total, slot % offset_total
    return side, k, row - offset_at(k) if side else row + offset_at(k)


def in_vmem(value):
    return pltpu.with_memory_space_constraint(value, pltpu.VMEM)


def part_top(pair, parts):
    top = pair % 2 * HALF_CH
    return top if parts == 2 else top + pair // 2 % 2 * (HALF_CH // 2)


def flag_at(slots, parts):
    return (1 + slots) * 2 * (BLOCK_CH // parts)


def read_info(info_ref, offset_total):
    lane = lax.broadcasted_iota(jnp.int32, (FLAG_ROWS, BINS), 1)
    at = lambda index: jnp.max(jnp.where(lane == index, info_ref[...], 0.0)).astype(jnp.int32)
    return [at(FLAG_ROWS + k) for k in range(offset_total)], [at(k) for k in range(offset_total)]


def pack(pieces, info, offset_total, group, turns):
    slots = slot_total(group, offset_total)
    piece_blocks = pieces[0].shape[0]

    def kernel(info_ref, *refs):
        piece_refs, out_refs, held = refs[: len(pieces)], refs[len(pieces) : -1], refs[-1]
        own_row, pair = lax.axis_index("blk"), lax.axis_index("pair")
        for turn, piece_ref in enumerate(piece_refs):
            first = (pair ^ turn) * piece_blocks
            for block in range(piece_blocks):
                held[first + block] = piece_ref[block]
        offsets, _ = read_info(info_ref, offset_total)
        flags = info_ref[...].astype(jnp.bfloat16)

        def fill(row, out_ref, parts):
            count = BLOCK_CH // parts
            top = pl.multiple_of(part_top(pair, parts) - part_top(pair, 2), count)
            blocks = [row]
            for slot in range(slots):
                _, _, partner = slot_pair(row, slot, lambda k: offsets[k], group, offset_total)
                blocks.append(jnp.clip(partner, 0, group - 1))
            for index, block in enumerate(blocks):
                for part in range(2):
                    at = (2 * index + part) * count
                    out_ref[at : at + count] = held[block, part, pl.ds(top, count)]
            out_ref[flag_at(slots, parts) :] = flags

        if turns:
            for (turn, parts), out_ref in zip(turns, out_refs):
                fill(own_row ^ turn, out_ref, parts)
        else:

            @pl.loop(0, group)
            def _(row):
                fill(row, out_refs[0].at[row], 2)

    def shape(parts):
        return (flag_at(slots, parts) + FLAG_ROWS, BINS)

    if turns:
        out_shape = [pltpu.VMEM(shape(parts), jnp.bfloat16) for _, parts in turns]
    else:
        out_shape = [jax.ShapeDtypeStruct((group,) + shape(2), jnp.bfloat16)]
    return pl.pallas_call(
        kernel,
        in_specs=[VMEM_SPEC] * (1 + len(pieces)),
        out_specs=[VMEM_SPEC] * len(out_shape),
        out_shape=out_shape,
        scratch_shapes=[pltpu.VMEM((group, 2, HALF_CH, BINS), jnp.bfloat16)],
        name="pack",
    )(*[in_vmem(value) for value in [info, *pieces]])


def top_of(tile):
    return jnp.max(jnp.max(tile, axis=1, keepdims=True), axis=0, keepdims=True)


def describe_slots(row, duo, offsets, sides, far_side, group, offset_total):
    found = []
    for a in range(2):
        side, k, other = 0, 0, 0
        for b in range(slot_total(group, offset_total) // 2):
            here = slot_pair(row, 2 * b + a, lambda j: offsets[j], group, offset_total)
            side, k, other = [jnp.where(duo == b, x, y) for x, y in zip(here, (side, k, other))]
        valid = jnp.logical_and(other >= 0, other < group)
        far = far_side(jnp.clip(other, 0, group - 1), k)
        own_side = sides[0]
        for j in range(1, offset_total):
            own_side = jnp.where(k == j, sides[j], own_side)
        sign = jnp.where(side == 0, 1.0 - 2.0 * own_side.astype(jnp.float32), 2.0 * far - 1.0)
        found.append((side, k, valid, jnp.max(sign) > 0.0, sign))
    return found


def fill_factors(segments, slot_list, duo, pair, tables, left, right):
    cos_mid, sin_mid, away = tables
    span = away.shape[1]
    c_mid, s_mid = cos_mid[pl.ds(pair, 1)], sin_mid[pl.ds(pair, 1)]
    for seg, parts in enumerate(segments):
        count = BLOCK_CH // len(parts)
        for turn, ref in enumerate(parts):
            top = pl.multiple_of(part_top(pair ^ turn, len(parts)), count)

            def put(target, part, block, value):
                rows = pl.ds(block * BLOCK_CH + top, count)
                target[seg][part, rows] = value.astype(jnp.bfloat16)

            real, imag = ref[:count].astype(jnp.float32), ref[count : 2 * count].astype(jnp.float32)
            for m in range(span):
                c, s, minus = [away[a, m : m + 1] for a in range(3)]
                put(left, 0, m, real * c)
                put(left, 1, m, imag * c)
                put(left, 0, span + m, imag * minus)
                put(left, 1, span + m, real * s)
            for a, (_, _, _, _, sign) in enumerate(slot_list):
                start = pl.multiple_of((2 * duo + a + 1) * 2 * count, 2 * count)
                real = ref[pl.ds(start, count)].astype(jnp.float32)
                imag = ref[pl.ds(start + count, count)].astype(jnp.float32)
                s = s_mid * sign
                put(right, 0, a, real * c_mid - imag * s)
                put(right, 1, a, imag * c_mid + real * s)


def contract(left, right):
    wide = lambda refs: jnp.concatenate([ref[part] for ref in refs for part in range(2)], axis=1)
    return lax.dot_general(
        wide(left), wide(right), (((1,), (1,)), ((), ())), preferred_element_type=jnp.float32
    )


def lag_values(total, a, span, turned, put):
    columns = slice(a * BLOCK_CH, (a + 1) * BLOCK_CH)

    def rows(at):
        return total[at * BLOCK_CH : (at + 1) * BLOCK_CH, columns]

    for m in range(span):
        even, odd = rows(m), rows(span + m)
        for lag, plus in ((span - 1 - m, not turned), (span + m, turned)):
            value = even + odd if plus else even - odd
            put(lag, (value.T if turned else value).astype(jnp.bfloat16))


def factor_scratch(segs, span):
    return [
        [pltpu.VMEM((2, 2 * span * BLOCK_CH, BINS), jnp.bfloat16)] * segs,
        [pltpu.VMEM((2, 2 * BLOCK_CH, BINS), jnp.bfloat16)] * segs,
    ]


def correlate_all(mine, theirs, info, offset_total, group, pairs):
    slots = slot_total(group, offset_total)
    segs = mine.shape[0]
    steps = segs // SEGS_PER_STEP
    lag_local = LAGS // pairs
    span = lag_local // 2
    normalizer = 1.0 / math.sqrt(segs * BINS)
    total_shape = (2 * span * BLOCK_CH, 2 * BLOCK_CH)

    def kernel(info_ref, *refs):
        offsets, sides = read_info(info_ref, offset_total)
        tables, (mine_ref, theirs_ref, flags_ref, first_ref, second_ref, left, right, total) = refs[:3], refs[3:]
        duo, step = pl.program_id(0), pl.program_id(1)
        row, pair = lax.axis_index("blk"), lax.axis_index("pair")
        lane = lax.broadcasted_iota(jnp.int32, (FLAG_ROWS, BINS), 1)

        def far_side(other, k):
            return top_of(jnp.where(lane == k, flags_ref[other].astype(jnp.float32), 0.0))

        found = describe_slots(row, duo, offsets, sides, far_side, group, offset_total)

        @pl.when(jnp.logical_and(duo == 0, step == 0))
        def _():
            first_ref[...] = jnp.zeros_like(first_ref)
            second_ref[...] = jnp.zeros_like(second_ref)

        segments = [(mine_ref.at[a], theirs_ref.at[a]) for a in range(SEGS_PER_STEP)]
        fill_factors(segments, found, duo, pair, tables, left, right)
        product = contract(left, right)

        @pl.when(step == 0)
        def _():
            total[...] = product

        @pl.when(step > 0)
        def _():
            total[...] += product

        for a, (side, k, valid, own_source, _) in enumerate(found):
            for a_side, out_ref in enumerate((first_ref, second_ref)):
                for turned in (False, True):
                    here = jnp.logical_and(valid, step == steps - 1)
                    here = jnp.logical_and(here, side == a_side)
                    here = jnp.logical_and(here, own_source != turned)

                    @pl.when(here)
                    def _():
                        def put(lag, value):
                            out_ref[0, k, lag] = value

                        lag_values(total, a, span, turned, put)

    out_shape = (1, offset_total, lag_local, BLOCK_CH, BLOCK_CH)
    out_spec = pl.BlockSpec(out_shape, lambda a, b: (0, 0, 0, 0, 0))
    flag_block = flag_at(slots, 2) // FLAG_ROWS
    piece = pl.BlockSpec((SEGS_PER_STEP,) + mine.shape[1:], lambda a, b: (b, 0, 0))
    flags = pl.BlockSpec((segs, FLAG_ROWS, BINS), lambda a, b: (0, flag_block, 0))
    return pl.pallas_call(
        kernel,
        grid=(slots // 2, steps),
        in_specs=[VMEM_SPEC] * 4 + [piece, piece, flags],
        out_specs=[out_spec] * 2,
        out_shape=[jax.ShapeDtypeStruct(out_shape, jnp.bfloat16)] * 2,
        scratch_shapes=factor_scratch(SEGS_PER_STEP, span) + [pltpu.VMEM(total_shape, jnp.float32)],
        name="correlate",
    )(in_vmem(info), *lag_tables(pairs, normalizer), mine, theirs, mine)


def join(groups):
    arrays = [array for group in groups for array in group]
    counts = [len(group) for group in groups]

    def kernel(*refs):
        sources, targets = refs[: len(arrays)], refs[len(arrays) :]
        for count, target in zip(counts, targets):
            at = 0
            for source in sources[:count]:
                target[at : at + source.shape[0]] = source[...]
                at += source.shape[0]
            sources = sources[count:]

    out_shape = [
        pltpu.VMEM((sum(array.shape[0] for array in group), BINS), jnp.bfloat16) for group in groups
    ]
    return pl.pallas_call(
        kernel,
        in_specs=[VMEM_SPEC] * len(arrays),
        out_specs=[VMEM_SPEC] * len(groups),
        out_shape=out_shape,
        name="join",
    )(*[in_vmem(array) for array in arrays])


def correlate_turns(turns, segments, info, offset_total, group, pairs):
    slots = slot_total(group, offset_total)
    lag_local = LAGS // pairs
    span = lag_local // 2
    normalizer = 1.0 / math.sqrt(len(turns) * BINS)
    total_shape = (2 * span * BLOCK_CH, 2 * BLOCK_CH)
    out_shape = (1, offset_total, lag_local, BLOCK_CH, BLOCK_CH)
    arrays = []
    for parts in segments:
        arrays += [array for array, _ in parts if all(array is not other for other in arrays)]
    index_of = lambda array: [array is other for other in arrays].index(True)
    places = [[(index_of(array), at) for array, at in parts] for parts in segments]

    def kernel(info_ref, *refs):
        offsets, sides = read_info(info_ref, offset_total)
        tables, refs = refs[:3], refs[3:]
        held = []
        for parts in places:
            rows = flag_at(slots, len(parts)) + FLAG_ROWS
            held.append([refs[index].at[at : at + rows] for index, at in parts])
        refs = refs[len(arrays) :]
        first_hbm, second_hbm, left, right, total, result, zeros, sems, zero_sems = refs
        row, pair = lax.axis_index("blk"), lax.axis_index("pair")
        lane = lax.broadcasted_iota(jnp.int32, (FLAG_ROWS, BINS), 1)

        def far_side(other, k):
            flags = jnp.zeros((FLAG_ROWS, BINS), jnp.float32)
            for (turn, _), parts in zip(turns, held):
                piece = parts[0][flag_at(slots, len(parts)) :].astype(jnp.float32)
                flags = jnp.where(row ^ turn == other, piece, flags)
            return top_of(jnp.where(lane == k, flags, 0.0))

        found = describe_slots(row, 0, offsets, sides, far_side, group, offset_total)

        slabs = []
        for side, out_hbm in enumerate((first_hbm, second_hbm)):
            for k in range(offset_total):
                pair_row = row - offsets[k] if side else row + offsets[k]
                is_pair = jnp.logical_and(pair_row >= 0, pair_row < group)
                copy = pltpu.make_async_copy(zeros, out_hbm.at[0, k], zero_sems.at[side, k])
                slabs.append((jnp.logical_not(is_pair), copy))
        zeros[...] = jnp.zeros_like(zeros)
        for blank, copy in slabs:
            pl.when(blank)(copy.start)

        def copy_to(out_hbm, a, k, lag):
            return pltpu.make_async_copy(result.at[a, lag], out_hbm.at[0, k, lag], sems.at[a, lag])

        fill_factors(held, found, 0, pair, tables, left, right)
        total[...] = contract(left, right)

        for a, (side, k, valid, own_source, _) in enumerate(found):
            for turned in (False, True):

                @pl.when(jnp.logical_and(valid, own_source != turned))
                def _():
                    def put(lag, value):
                        result[a, lag] = value
                        pl.when(side == 0)(copy_to(first_hbm, a, k, lag).start)
                        pl.when(side != 0)(copy_to(second_hbm, a, k, lag).start)

                    lag_values(total, a, span, turned, put)

        for a, (side, k, valid, own_source, _) in enumerate(found):

            @pl.when(valid)
            def _():
                for lag in range(lag_local):
                    copy_to(first_hbm, a, 0, lag).wait()

        for blank, copy in slabs:
            pl.when(blank)(copy.wait)

    any_spec = pl.BlockSpec(memory_space=pl.ANY)
    operands = [in_vmem(array) for array in arrays]
    return pl.pallas_call(
        kernel,
        in_specs=[VMEM_SPEC] * (4 + len(operands)),
        out_specs=[any_spec] * 2,
        out_shape=[jax.ShapeDtypeStruct(out_shape, jnp.bfloat16)] * 2,
        scratch_shapes=factor_scratch(len(turns), span)
        + [
            pltpu.VMEM(total_shape, jnp.float32),
            pltpu.VMEM((2, lag_local, BLOCK_CH, BLOCK_CH), jnp.bfloat16),
            pltpu.VMEM((lag_local, BLOCK_CH, BLOCK_CH), jnp.bfloat16),
            pltpu.SemaphoreType.DMA((2, lag_local)),
            pltpu.SemaphoreType.DMA((2, offset_total)),
        ],
        name="correlate",
    )(*[in_vmem(value) for value in [info, *lag_tables(pairs, normalizer)]], *operands)


def local(records, offsets, source_side):
    group, pairs = lax.axis_size("blk"), lax.axis_size("pair")
    half_of = lambda pair: pair % 2
    assert records.shape[0] == 1

    def swap(value, axis, turn):
        return lax.ppermute(value, axis, [(a, a ^ turn) for a in range(lax.axis_size(axis))])

    offset_total = offsets.shape[0]
    traces = records.reshape(records.shape[1], SAMPLES)
    mine, other, info = whiten(traces, offsets, source_side, half_of)
    pieces = [mine]
    for turn in range(1, pairs):
        pieces.append(swap(other if turn % 2 else mine, "pair", turn))
    turns = turns_of(group, pairs)
    packed = pack(pieces, info, offset_total, group, turns)
    if not turns:
        arrived = lax.all_to_all(packed[0], "blk", split_axis=0, concat_axis=0, tiled=True)
        theirs = swap(arrived, "pair", 1)
        return correlate_all(arrived, theirs, info, offset_total, group, pairs)
    parts_of = dict(turns)
    arrived = {}
    for (turn, _), value in zip(turns, packed):
        arrived[turn] = swap(value, "blk", turn) if turn else value
    quarters = [turn for turn in JOINED if parts_of[turn] == 4]
    below, both = join([[arrived[turn] for turn in quarters], [arrived[turn] for turn in JOINED]])
    below_2 = swap(below, "pair", 2)
    both_1 = swap(both, "pair", 1)
    below_3 = swap(below_2, "pair", 1)
    segments = []
    for turn, parts in turns:
        if turn in JOINED:
            ahead = JOINED[: JOINED.index(turn)]
            found = [(arrived[turn], 0), (both_1, sum(arrived[other].shape[0] for other in ahead))]
            if parts == 4:
                at = sum(arrived[other].shape[0] for other in ahead if other in quarters)
                found += [(below_2, at), (below_3, at)]
        else:
            hops = [swap(arrived[turn], "pair", hop) for hop in range(1, parts)]
            found = [(array, 0) for array in [arrived[turn]] + hops]
        segments.append(found)
    return correlate_turns(turns, segments, info, offset_total, group, pairs)


def turns_of(group, pairs):
    return TURNS if group == len(TURNS) and pairs == 4 else ()


def solution(mesh):
    placed = (P("blk", "pair", None), P(), P("blk", None))

    return jax.shard_map(
        local,
        mesh=mesh,
        in_specs=placed,
        out_specs=(P("blk", None, "pair", None, None), P("blk", None, "pair", None, None)),
        check_vma=False,
    )
```
